256 devices in a mesh: ctx: 256 (over y, x, z, core).
Axes of the slice: x: 4, y: 4, z: 8, core: 2. Of those that a mesh axis runs over, the one named last changes fastest.
Arguments:
- query_rows: bfloat16 [32768, 1024], P('ctx'), may hold values from -12 to 12
- key_rows: bfloat16 [32768, 1024], P('ctx'), may hold values from -6 to 6
- value_rows: bfloat16 [32768, 1024], P('ctx'), may hold values from -6 to 6
- out_grad: bfloat16 [32768, 1024], P('ctx'), may hold values from -192 to 192
- inputs: bfloat16 [32768, 2048], P('ctx'), may hold values from -24 to 24
Outputs:
- query_grad: bfloat16 [32768, 1024], P('ctx')
- key_grad: bfloat16 [32768, 1024], P('ctx')
- value_grad: bfloat16 [32768, 1024], P('ctx')
- weight_grad: float32 [2048, 1024], P('ctx')
The draws below stay inside these ranges and needn't reach their ends.
All inputs are finite; a program needn't handle non-finite values.
Results may differ from the reference program's by a relative error of at most 0.015.
Values may be sent and summed in bfloat16 or wider, within the bound.
No kernel may reach another device: no remote copies, remote signals or barrier semaphores. Data moves between devices by JAX's collectives and lax.ppermute only.
A program may use at most 128 MiB of HBM per device.

```python
import math
import jax
import jax.numpy as jnp
from jax import lax

D = 2048
HEADS = 8
HEAD = 128
SPAN = 2
TOK_DEV = 128
TOKENS = 32768
N_CTX = 256


def draw_query_rows(key, part):
    noise_draw = jax.random.normal(jax.random.fold_in(key, 11), (TOKENS, HEADS * HEAD), jnp.float32)
    values = jnp.clip(noise_draw, -4.0, 4.0)
    return values.astype(jnp.bfloat16)


def draw_key_rows(key, part):
    noise_draw = jax.random.normal(jax.random.fold_in(key, 13), (TOKENS, HEADS * HEAD), jnp.float32)
    values = jnp.clip(noise_draw, -4.0, 4.0)
    return values.astype(jnp.bfloat16)


def spiked(entries, own_key, source, target, blocks, factor):
    def block_of(dim):
        return (jnp.arange(entries.shape[dim]) // (entries.shape[dim] // blocks)).reshape((-1,) + (1,) * (entries.ndim - 1 - dim))

    first = jax.random.permutation(own_key, blocks)[block_of(target)]
    other_side = (block_of(target) + blocks // 2) % blocks
    return jnp.where((block_of(source) == first) | (block_of(source) == other_side), factor * entries, entries)


def block_levels(rng, shape, split, smallest, top_value):
    def one(axis_at, parts):
        steps = jax.random.uniform(jax.random.fold_in(jax.random.fold_in(rng, 6), axis_at), (parts,), jnp.float32, smallest / len(split), top_value / len(split))
        return jnp.repeat(jnp.exp(steps), shape[axis_at] // parts).reshape((-1,) + (1,) * (len(shape) - axis_at - 1))

    gain = one(*split[0])
    for cut in split[1:]:
        gain = gain * one(*cut)
    return gain


def scatter_about(own_key, dims, scale, most, shards=(), kind=jnp.bfloat16):
    result = scale * jax.random.normal(own_key, dims, jnp.float32)
    if shards:
        result = result * block_levels(own_key, dims, shards, -0.22, 0.18)
    return jnp.clip(result, -most, most).astype(kind)


def heavy_noise(rng, shape, deviation, bound, pieces, heavy, kind=jnp.bfloat16):
    drawn = deviation * jax.random.normal(rng, shape, jnp.float32)
    if pieces:
        drawn = drawn * block_levels(rng, shape, pieces, -0.22, 0.18)
    return jnp.clip(spiked(drawn, jax.random.fold_in(rng, 3), *heavy), -bound, bound).astype(kind)


def setup_inputs(seed: int = 0) -> dict:
    keys = jax.random.split(jax.random.key(seed), 6)
    return {
        "query_rows": draw_query_rows(jax.random.fold_in(keys[5], 71), 0),
        "key_rows": draw_key_rows(jax.random.fold_in(keys[5], 71), 0),
        "value_rows": scatter_about(keys[2], (TOKENS, HEADS * HEAD), 1.0, 6.0, ((0, 256),)),
        "out_grad": scatter_about(keys[3], (TOKENS, HEADS * HEAD), 32.0, 192.0, ((0, 256),)),
        "inputs": heavy_noise(keys[4], (TOKENS, D), 1.0, 24.0, ((0, 256),), (0, 1, 256, 6.0)),
    }


def reference(query_rows, key_rows, value_rows, out_grad, inputs):
    features = HEADS * HEAD
    window = 2 * SPAN + 1
    score_scale = 1.0 / math.sqrt(HEAD)
    query_blocks = query_rows.reshape(N_CTX, TOK_DEV, HEADS, HEAD)
    key_blocks = key_rows.reshape(N_CTX, TOK_DEV, HEADS, HEAD)
    value_blocks = value_rows.reshape(N_CTX, TOK_DEV, HEADS, HEAD)
    grad_blocks = out_grad.reshape(N_CTX, TOK_DEV, HEADS, HEAD)
    offsets = jnp.arange(-SPAN, SPAN + 1, dtype=jnp.int32)

    def shard_step(carry, shard):
        key_sum, value_sum = carry
        targets = ((shard + offsets) % N_CTX).astype(jnp.int32)
        key_window = key_blocks[targets].reshape(window * TOK_DEV, HEADS, HEAD).astype(jnp.float32)
        value_window = value_blocks[targets].reshape(window * TOK_DEV, HEADS, HEAD).astype(jnp.float32)
        query_heads = query_blocks[shard].astype(jnp.float32)
        grad_heads = grad_blocks[shard].astype(jnp.float32)
        scores = jnp.einsum('thd,uhd->htu', query_heads, key_window) * score_scale
        row_max = lax.optimization_barrier(jnp.max(scores, axis=2, keepdims=True))
        log_total = row_max + jnp.log(lax.optimization_barrier(jnp.sum(jnp.exp(scores - row_max), axis=2, keepdims=True)))
        probs = jnp.exp(scores - log_total)
        prob_low = probs.astype(jnp.bfloat16)
        attended = jnp.einsum('htu,uhd->thd', prob_low.astype(jnp.float32), value_window)
        row_delta = jnp.einsum('thd,thd->ht', grad_heads, attended)
        grad_probs = jnp.einsum('thd,uhd->htu', grad_heads, value_window)
        grad_scores = probs * (grad_probs - row_delta[:, :, None])
        score_low = grad_scores.astype(jnp.bfloat16).astype(jnp.float32)
        query_grad = (jnp.einsum('htu,uhd->thd', score_low, key_window) * score_scale).astype(jnp.bfloat16)
        key_terms = (jnp.einsum('htu,thd->uhd', score_low, query_heads) * score_scale).astype(jnp.bfloat16)
        value_terms = jnp.einsum('htu,thd->uhd', prob_low.astype(jnp.float32), grad_heads).astype(jnp.bfloat16)
        key_terms = key_terms.reshape(window, TOK_DEV, features).astype(jnp.float32)
        value_terms = value_terms.reshape(window, TOK_DEV, features).astype(jnp.float32)
        key_sum = key_sum.at[targets].add(key_terms)
        value_sum = value_sum.at[targets].add(value_terms)
        return ((key_sum, value_sum), query_grad.reshape(TOK_DEV, features))
    zero_sums = jnp.zeros((N_CTX, TOK_DEV, features), jnp.float32)
    (key_sum, value_sum), query_grad = lax.scan(shard_step, (zero_sums, zero_sums), jnp.arange(N_CTX, dtype=jnp.int32))
    query_grad = query_grad.reshape(TOKENS, features)
    key_grad = key_sum.reshape(TOKENS, features).astype(jnp.bfloat16)
    value_grad = value_sum.reshape(TOKENS, features).astype(jnp.bfloat16)
    weight_grad = jnp.dot(inputs.T, value_grad, preferred_element_type=jnp.float32) * (1.0 / math.sqrt(TOKENS))
    return (query_grad, key_grad, value_grad, weight_grad)
```

```python
import math

import jax
import jax.numpy as jnp
from jax import lax
from jax.experimental import pallas as pl
from jax.experimental.pallas import tpu as pltpu
from jax.sharding import Mesh, PartitionSpec as P

HEAD = 128
NEG = -1e30


AXES = ("y", "x", "z", "c")
LAST = (((1,), (1,)), ((), ()))
FIRST = (((0,), (0,)), ((), ()))


def physical_mesh(mesh):
    count = mesh.devices.size
    sizes = (4, 4, 8, 2) if count == 256 else (2, count // 8, 2, 2)
    return Mesh(mesh.devices.reshape(sizes), AXES)


def to_chip(array, count, step, cross):
    pairs = []
    for device in range(count):
        chip, core = device // 2, device % 2
        pairs.append((device, (chip + step) % (count // 2) * 2 + (core ^ cross)))
    return lax.ppermute(array, AXES, pairs)


def along_x(array, sizes, step):
    ny, nx, nz, nc = sizes
    pairs = []
    for y in range(ny):
        for x in range(nx):
            for rest in range(nz * nc):
                pairs.append(
                    ((y * nx + x) * nz * nc + rest, (y * nx + (x + step) % nx) * nz * nc + rest)
                )
    return lax.ppermute(array, AXES, pairs)


def pack_kernel(core, q_o, do_o, k_m, v_m, k_o, v_o, kv_m, kv_o, qdo_o):
    kv_m[0] = k_m[...]
    kv_m[1] = v_m[...]
    kv_o[0] = k_o[...]
    kv_o[1] = v_o[...]
    qdo_o[0] = q_o[...]
    qdo_o[1] = do_o[...]


def pack(core, query, key, value, grad):
    rows, features = query.shape
    half = features // 2
    mine = pl.BlockSpec((rows, half), lambda i, c: (0, c[0]))
    other = pl.BlockSpec((rows, half), lambda i, c: (0, 1 - c[0]))
    whole = pl.BlockSpec((2, rows, half), lambda i, c: (0, 0, 0))
    pair = jax.ShapeDtypeStruct((2, rows, half), query.dtype)
    return pl.pallas_call(
        pack_kernel,
        out_shape=(pair, pair, pair),
        grid_spec=pltpu.PrefetchScalarGridSpec(
            num_scalar_prefetch=1,
            grid=(1,),
            in_specs=[other, other, mine, mine, other, other],
            out_specs=(whole, whole, whole),
        ),
        name="pack",
    )(core, query, grad, key, value, key, value)


def scores_of(core, keys, queries, scale):
    flat = lax.dot_general(keys, queries, LAST, preferred_element_type=jnp.float32) * scale
    size = flat.shape[0] // 6
    tokens = queries.shape[0] // 2
    first = lax.broadcasted_iota(jnp.int32, (1, 2 * tokens), 1) < tokens
    even = core == 0
    bias = {
        0: jnp.where(jnp.logical_and(even, jnp.logical_not(first)), NEG, 0.0),
        1: jnp.where(jnp.logical_and(jnp.logical_not(even), first), NEG, 0.0),
        4: jnp.where(jnp.logical_and(jnp.logical_not(even), jnp.logical_not(first)), NEG, 0.0),
        5: jnp.where(jnp.logical_and(even, first), NEG, 0.0),
    }
    parts = []
    for block in range(6):
        part = flat[block * size : (block + 1) * size]
        parts.append(part + bias[block] if block in bias else part)
    return jnp.concatenate(parts, 0)


def value_kernel(scale, core, q, qp, do, dop, k0, k1, k2, k3, k4, k5, prev, own, after, lse):
    queries = jnp.concatenate([q[...], qp[...]], 0)
    grads = jnp.concatenate([do[...], dop[...]], 0)
    keys = jnp.concatenate([k0[...], k1[...], k2[...], k3[...], k4[...], k5[...]], 0)
    scores = scores_of(core[0], keys, queries, scale)
    top = jnp.max(scores, axis=0, keepdims=True)
    raised = jnp.exp(scores - top)
    total = jnp.sum(raised, axis=0, keepdims=True)
    probs = (raised * (1.0 / total)).astype(jnp.bfloat16)
    terms = jnp.dot(probs, grads, preferred_element_type=jnp.float32)
    two = terms.shape[0] // 3
    prev[...] = terms[:two].astype(jnp.bfloat16)
    own[...] = terms[two : 2 * two]
    after[...] = terms[2 * two :].astype(jnp.bfloat16)
    lse[...] = jnp.broadcast_to(top + jnp.log(total), lse.shape)


def score_kernel(
    scale, core, q, qp, do, dop, k0, k1, k2, k3, k4, k5, v0, v1, v2, v3, v4, v5, lse,
    dq, dqp, prev, own, after,
):
    queries = jnp.concatenate([q[...], qp[...]], 0)
    grads = jnp.concatenate([do[...], dop[...]], 0)
    keys = jnp.concatenate([k0[...], k1[...], k2[...], k3[...], k4[...], k5[...]], 0)
    values = jnp.concatenate([v0[...], v1[...], v2[...], v3[...], v4[...], v5[...]], 0)
    scores = scores_of(core[0], keys, queries, scale)
    probs = jnp.exp(scores - lse[0:1])
    grad_probs = lax.dot_general(values, grads, LAST, preferred_element_type=jnp.float32)
    rounded = probs.astype(jnp.bfloat16).astype(jnp.float32)
    delta = jnp.sum(rounded * grad_probs, axis=0, keepdims=True)
    low = (probs * (grad_probs - delta)).astype(jnp.bfloat16)
    query_t = lax.dot_general(keys, low, FIRST, preferred_element_type=jnp.float32) * scale
    query = query_t.T.astype(jnp.bfloat16)
    tokens = query.shape[0] // 2
    dq[...] = query[:tokens]
    dqp[...] = query[tokens:]
    terms = jnp.dot(low, queries, preferred_element_type=jnp.float32) * scale
    two = terms.shape[0] // 3
    prev[...] = terms[:two].astype(jnp.bfloat16)
    own[...] = terms[two : 2 * two]
    after[...] = terms[2 * two :].astype(jnp.bfloat16)


def attention_specs(rows, heads):
    mine = pl.BlockSpec((rows, HEAD), lambda h, c: (0, c[0] * heads + h))
    first = pl.BlockSpec((None, rows, HEAD), lambda h, c: (0, 0, h))
    second = pl.BlockSpec((None, rows, HEAD), lambda h, c: (1, 0, h))
    terms = pl.BlockSpec((2 * rows, HEAD), lambda h, c: (0, h))
    stats = pl.BlockSpec((None, 8, 2 * rows), lambda h, c: (h, 0, 0))
    one = pl.BlockSpec((rows, HEAD), lambda h, c: (0, h))
    return mine, first, second, terms, stats, one


def value_pass(core, query, grad, part_qdo, windows, scale):
    rows, features = query.shape
    heads = features // HEAD // 2
    mine, first, second, terms, stats, _ = attention_specs(rows, heads)
    low = jax.ShapeDtypeStruct((2 * rows, heads * HEAD), jnp.bfloat16)
    high = jax.ShapeDtypeStruct((2 * rows, heads * HEAD), jnp.float32)
    work = heads * 2 * rows * 6 * rows
    return pl.pallas_call(
        lambda *refs: value_kernel(scale, *refs),
        out_shape=(low, high, low, jax.ShapeDtypeStruct((heads, 8, 2 * rows), jnp.float32)),
        grid_spec=pltpu.PrefetchScalarGridSpec(
            num_scalar_prefetch=1,
            grid=(heads,),
            in_specs=[mine, first, mine, second] + [first] * 6,
            out_specs=(terms, terms, terms, stats),
        ),
        cost_estimate=pl.CostEstimate(
            flops=4 * work * HEAD, transcendentals=work, bytes_accessed=4 << 20
        ),
        name="value_pass",
    )(core, query, part_qdo, grad, part_qdo, *windows)


def score_pass(core, query, grad, part_qdo, windows, lse, scale):
    rows, features = query.shape
    heads = features // HEAD // 2
    mine, first, second, terms, stats, one = attention_specs(rows, heads)
    low = jax.ShapeDtypeStruct((2 * rows, heads * HEAD), jnp.bfloat16)
    high = jax.ShapeDtypeStruct((2 * rows, heads * HEAD), jnp.float32)
    part = jax.ShapeDtypeStruct((rows, heads * HEAD), jnp.bfloat16)
    work = heads * 2 * rows * 6 * rows
    return pl.pallas_call(
        lambda *refs: score_kernel(scale, *refs),
        out_shape=(part, part, low, high, low),
        grid_spec=pltpu.PrefetchScalarGridSpec(
            num_scalar_prefetch=1,
            grid=(heads,),
            in_specs=[mine, first, mine, second] + [first] * 6 + [second] * 6 + [stats],
            out_specs=(one, one, terms, terms, terms),
        ),
        cost_estimate=pl.CostEstimate(
            flops=8 * work * HEAD, transcendentals=work, bytes_accessed=6 << 20
        ),
        name="score_pass",
    )(core, query, part_qdo, grad, part_qdo, *windows, *windows, lse)


def weight_kernel(count, place, same, part, *rest):
    gathered, out = rest[:count], rest[count]
    rows = same.shape[1]
    total = jnp.zeros(out.shape, jnp.float32)
    for step in range(count):
        source = lax.rem(place[0] - step + count, count)
        total += lax.dot_general(
            same[source], gathered[step][:rows], FIRST, preferred_element_type=jnp.float32
        )
        total += lax.dot_general(
            part[source], gathered[step][rows:], FIRST, preferred_element_type=jnp.float32
        )
    out[...] = total.astype(jnp.bfloat16)


def weight_pass(place, same, part, gathered):
    count, rows, width = same.shape
    columns = gathered[0].shape[1]
    tile = 256
    inputs = pl.BlockSpec((count, rows, tile), lambda i, c: (0, 0, i))
    grads = pl.BlockSpec((2 * rows, columns), lambda i, c: (0, 0))
    return pl.pallas_call(
        lambda *refs: weight_kernel(count, *refs),
        out_shape=jax.ShapeDtypeStruct((width, columns), jnp.bfloat16),
        grid_spec=pltpu.PrefetchScalarGridSpec(
            num_scalar_prefetch=1,
            grid=(width // tile,),
            in_specs=[inputs, inputs] + [grads] * count,
            out_specs=pl.BlockSpec((tile, columns), lambda i, c: (i, 0)),
        ),
        cost_estimate=pl.CostEstimate(
            flops=4 * count * rows * width * columns, transcendentals=0, bytes_accessed=4 << 20
        ),
        name="weight_pass",
    )(place, same, part, *gathered)


def local(query_rows, key_rows, value_rows, out_grad, inputs):
    rows, features = query_rows.shape
    sizes = tuple(lax.axis_size(name) for name in AXES)
    ny, nx, nz, nc = sizes
    devices = ny * nx * nz * nc
    scale = 1.0 / math.sqrt(HEAD)
    core_at = lax.axis_index("c")
    core = core_at.astype(jnp.int32)[None]
    place = lax.axis_index("x").astype(jnp.int32)[None]
    even = core_at == 0

    def both_halves(mine, other):
        return jnp.where(
            even, jnp.concatenate([mine, other], 1), jnp.concatenate([other, mine], 1)
        )

    kv_mine, kv_other, qdo_other = pack(core, query_rows, key_rows, value_rows, out_grad)
    kv_part = to_chip(kv_other, devices, 0, 1)
    qdo_part = to_chip(qdo_other, devices, 0, 1)
    next_same = to_chip(kv_mine, devices, -1, 0)
    next_cross = to_chip(kv_other, devices, -1, 1)
    prev_same = to_chip(kv_mine, devices, 1, 0)
    prev_cross = to_chip(kv_other, devices, 1, 1)
    windows = (prev_same, prev_cross, kv_mine, kv_part, next_same, next_cross)

    block = inputs.shape[1] // (ny * nx)
    split = inputs.reshape(rows, ny, nx, block).transpose(2, 0, 1, 3).reshape(nx, rows, ny * block)
    in_same = lax.all_to_all(split, "x", 0, 0, tiled=True)
    in_part = to_chip(in_same, devices, 0, 1)

    prev, own, after, lse = value_pass(core, query_rows, out_grad, qdo_part, windows, scale)
    from_next = to_chip(prev, devices, -1, 0)
    from_prev = to_chip(after, devices, 1, 0)
    dq, dq_other, key_prev, key_own, key_after = score_pass(
        core, query_rows, out_grad, qdo_part, windows, lse, scale
    )
    value_half = (own + from_next.astype(jnp.float32) + from_prev.astype(jnp.float32)).astype(
        jnp.bfloat16
    )
    gathered = [value_half] + [along_x(value_half, sizes, step) for step in range(1, nx)]
    key_from_next = to_chip(key_prev, devices, -1, 0)
    key_from_prev = to_chip(key_after, devices, 1, 0)
    value_back = to_chip(value_half[rows:], devices, 0, 1)
    query_back = to_chip(dq_other, devices, 0, 1)

    partial = weight_pass(place, in_same, in_part, gathered)
    half = features // 2
    own_count = inputs.shape[1] // devices
    pieces = partial.reshape(ny * nz * nc, own_count, half)
    arrived = lax.all_to_all(pieces, ("y", "z", "c"), 0, 0, tiled=True)
    summed = jnp.sum(
        arrived.reshape(ny * nz, nc, own_count, half).astype(jnp.float32), axis=0
    )
    weight_grad = summed.transpose(1, 0, 2).reshape(own_count, features) * (
        1.0 / math.sqrt(rows * devices)
    )

    key_half = (
        key_own + key_from_next.astype(jnp.float32) + key_from_prev.astype(jnp.float32)
    ).astype(jnp.bfloat16)
    key_back = to_chip(key_half[rows:], devices, 0, 1)
    query_grad = both_halves(dq, query_back)
    value_grad = both_halves(value_half[:rows], value_back)
    key_grad = both_halves(key_half[:rows], key_back)
    return (query_grad, key_grad, value_grad, weight_grad)


def solution(mesh):
    fine = physical_mesh(mesh)
    spec = P(AXES, None)
    return jax.shard_map(
        local,
        mesh=fine,
        in_specs=(spec,) * 5,
        out_specs=(spec,) * 4,
        check_vma=False,
    )
```

```python
import math

import jax
import jax.numpy as jnp
from jax import lax
from jax.experimental import pallas as pl
from jax.experimental.pallas import tpu as pltpu
from jax.sharding import Mesh, PartitionSpec as P

HEAD = 128
NEG = -1e30
ROOM = pltpu.CompilerParams(vmem_limit_bytes=20 << 20)


AXES = ("y", "x", "z", "c")
LAST = (((1,), (1,)), ((), ()))
FIRST = (((0,), (0,)), ((), ()))


def physical_mesh(mesh):
    count = mesh.devices.size
    sizes = (4, 4, 8, 2) if count == 256 else (2, count // 8, 2, 2)
    return Mesh(mesh.devices.reshape(sizes), AXES)


def to_chip(array, count, step, cross):
    pairs = []
    for device in range(count):
        chip, core = device // 2, device % 2
        pairs.append((device, (chip + step) % (count // 2) * 2 + (core ^ cross)))
    return lax.ppermute(array, AXES, pairs)


def along_x(array, sizes, step):
    ny, nx, nz, nc = sizes
    pairs = []
    for y in range(ny):
        for x in range(nx):
            for rest in range(nz * nc):
                pairs.append(
                    ((y * nx + x) * nz * nc + rest, (y * nx + (x + step) % nx) * nz * nc + rest)
                )
    return lax.ppermute(array, AXES, pairs)


def vmem(count):
    return [pl.BlockSpec(memory_space=pltpu.VMEM)] * count


def smem():
    return pl.BlockSpec(memory_space=pltpu.SMEM)


def pack_kernel(core, query, key, value, grad, mine, other):
    half = query.shape[1] // 2
    for side in range(2):
        low = side * half

        @pl.when(core[0] == side)
        def _():
            for at, source in enumerate((key, value, query, grad)):
                mine[at] = source[:, low : low + half]
                other[at] = source[:, half - low : 2 * half - low]


def pack(core, query, key, value, grad):
    rows, features = query.shape
    four = jax.ShapeDtypeStruct((4, rows, features // 2), query.dtype)
    return pl.pallas_call(
        pack_kernel,
        out_shape=(four, four),
        in_specs=[smem()] + vmem(4),
        out_specs=tuple(vmem(2)),
        compiler_params=ROOM,
        name="pack",
    )(core, query, key, value, grad)


def join_kernel(mine, part, key, value, query, grad):
    rows = mine.shape[1]
    for at, target in enumerate((key, value, query, grad)):
        target[:rows] = mine[at]
        target[rows:] = part[at]


def join(mine, part):
    _, rows, half = mine.shape
    two = jax.ShapeDtypeStruct((2 * rows, half), mine.dtype)
    return pl.pallas_call(
        join_kernel,
        out_shape=(two,) * 4,
        in_specs=vmem(2),
        out_specs=tuple(vmem(4)),
        compiler_params=ROOM,
        name="join",
    )(mine, part)


def window_bias(even, tokens):
    first = lax.broadcasted_iota(jnp.int32, (1, 2 * tokens), 1) < tokens
    odd, second = jnp.logical_not(even), jnp.logical_not(first)
    return {
        0: jnp.where(jnp.logical_and(even, second), NEG, 0.0),
        1: jnp.where(jnp.logical_and(odd, first), NEG, 0.0),
        4: jnp.where(jnp.logical_and(odd, second), NEG, 0.0),
        5: jnp.where(jnp.logical_and(even, first), NEG, 0.0),
    }


def scores_of(bias, keys, queries, scale):
    flat = lax.dot_general(keys, queries, LAST, preferred_element_type=jnp.float32) * scale
    size = flat.shape[0] // 6
    parts = []
    for block in range(6):
        part = flat[block * size : (block + 1) * size]
        parts.append(part + bias[block] if block in bias else part)
    return jnp.concatenate(parts, 0)


def value_kernel(scale, core, query, grad, before_k, key, after_k, prev, own, after, lse):
    two, width = query.shape
    bias = window_bias(core[0] == 0, two // 2)
    for head in range(width // HEAD):
        at = slice(head * HEAD, (head + 1) * HEAD)
        keys = jnp.concatenate([before_k[:, at], key[:, at], after_k[:, at]], 0)
        scores = scores_of(bias, keys, query[:, at], scale)
        top = jnp.max(scores, axis=0, keepdims=True)
        raised = jnp.exp(scores - top)
        total = jnp.sum(raised, axis=0, keepdims=True)
        probs = (raised * (1.0 / total)).astype(jnp.bfloat16)
        terms = jnp.dot(probs, grad[:, at], preferred_element_type=jnp.float32)
        prev[:, at] = terms[:two].astype(jnp.bfloat16)
        own[:, at] = terms[two : 2 * two]
        after[:, at] = terms[2 * two :].astype(jnp.bfloat16)
        lse[head] = jnp.broadcast_to(top + jnp.log(total), lse.shape[1:])


def score_kernel(
    scale, core, query, grad, before_k, key, after_k, before_v, value, after_v, lse,
    query_grad, query_back, prev, own, after,
):
    two, width = query.shape
    bias = window_bias(core[0] == 0, two // 2)
    for head in range(width // HEAD):
        at = slice(head * HEAD, (head + 1) * HEAD)
        keys = jnp.concatenate([before_k[:, at], key[:, at], after_k[:, at]], 0)
        values = jnp.concatenate([before_v[:, at], value[:, at], after_v[:, at]], 0)
        scores = scores_of(bias, keys, query[:, at], scale)
        probs = jnp.exp(scores - lse[head, 0:1])
        grad_probs = lax.dot_general(values, grad[:, at], LAST, preferred_element_type=jnp.float32)
        rounded = probs.astype(jnp.bfloat16).astype(jnp.float32)
        delta = jnp.sum(rounded * grad_probs, axis=0, keepdims=True)
        low = (probs * (grad_probs - delta)).astype(jnp.bfloat16)
        turned = lax.dot_general(keys, low, FIRST, preferred_element_type=jnp.float32) * scale
        found = turned.T.astype(jnp.bfloat16)
        query_grad[:, at] = found[: two // 2]
        query_back[:, at] = found[two // 2 :]
        terms = jnp.dot(low, query[:, at], preferred_element_type=jnp.float32) * scale
        prev[:, at] = terms[:two].astype(jnp.bfloat16)
        own[:, at] = terms[two : 2 * two]
        after[:, at] = terms[2 * two :].astype(jnp.bfloat16)


def value_pass(core, query, grad, keys, scale):
    two, width = query.shape
    heads = width // HEAD
    low = jax.ShapeDtypeStruct((two, width), jnp.bfloat16)
    high = jax.ShapeDtypeStruct((two, width), jnp.float32)
    work = heads * two * 3 * two
    return pl.pallas_call(
        lambda *refs: value_kernel(scale, *refs),
        out_shape=(low, high, low, jax.ShapeDtypeStruct((heads, 8, two), jnp.float32)),
        in_specs=[smem()] + vmem(5),
        out_specs=tuple(vmem(4)),
        cost_estimate=pl.CostEstimate(
            flops=4 * work * HEAD, transcendentals=work, bytes_accessed=4 << 20
        ),
        compiler_params=ROOM,
        name="value_pass",
    )(core, query, grad, *keys)


def score_pass(core, query, grad, keys, values, lse, scale):
    two, width = query.shape
    heads = width // HEAD
    low = jax.ShapeDtypeStruct((two, width), jnp.bfloat16)
    high = jax.ShapeDtypeStruct((two, width), jnp.float32)
    part = jax.ShapeDtypeStruct((two // 2, width), jnp.bfloat16)
    work = heads * two * 3 * two
    return pl.pallas_call(
        lambda *refs: score_kernel(scale, *refs),
        out_shape=(part, part, low, high, low),
        in_specs=[smem()] + vmem(9),
        out_specs=tuple(vmem(5)),
        cost_estimate=pl.CostEstimate(
            flops=8 * work * HEAD, transcendentals=work, bytes_accessed=6 << 20
        ),
        compiler_params=ROOM,
        name="score_pass",
    )(core, query, grad, *keys, *values, lse)


def block_kernel(count, groups, place, own, part, *blocks):
    rows, width = own.shape
    size = width // (groups * count)
    for step, block in enumerate(blocks):
        target = lax.rem(place[0] + step, count)
        for group in range(groups):
            start = pl.multiple_of((group * count + target) * size, size)
            at = slice(group * size, (group + 1) * size)
            block[:rows, at] = own[:, pl.ds(start, size)]
            block[rows:, at] = part[:, pl.ds(start, size)]


def input_blocks(place, own, part, count, groups):
    rows, width = own.shape
    block = jax.ShapeDtypeStruct((2 * rows, width // count), own.dtype)
    return pl.pallas_call(
        lambda *refs: block_kernel(count, groups, *refs),
        out_shape=(block,) * count,
        in_specs=[smem()] + vmem(2),
        out_specs=tuple(vmem(count)),
        compiler_params=ROOM,
        name="input_blocks",
    )(place, own, part)


def weight_kernel(count, *refs):
    inputs, gathered, out = refs[:count], refs[count : 2 * count], refs[2 * count]
    tile = 256
    for low in range(0, out.shape[0], tile):
        total = jnp.zeros((tile, out.shape[1]), jnp.float32)
        for step in range(count):
            total += lax.dot_general(
                inputs[step][:, low : low + tile],
                gathered[step][...],
                FIRST,
                preferred_element_type=jnp.float32,
            )
        out[low : low + tile] = total.astype(jnp.bfloat16)


def weight_pass(inputs, gathered):
    count = len(inputs)
    rows, width = inputs[0].shape
    columns = gathered[0].shape[1]
    return pl.pallas_call(
        lambda *refs: weight_kernel(count, *refs),
        out_shape=jax.ShapeDtypeStruct((width, columns), jnp.bfloat16),
        in_specs=vmem(2 * count),
        out_specs=pl.BlockSpec(memory_space=pltpu.VMEM),
        cost_estimate=pl.CostEstimate(
            flops=2 * count * rows * width * columns, transcendentals=0, bytes_accessed=4 << 20
        ),
        compiler_params=ROOM,
        name="weight_pass",
    )(*inputs, *gathered)


def local(query_rows, key_rows, value_rows, out_grad, inputs):
    rows, features = query_rows.shape
    sizes = tuple(lax.axis_size(name) for name in AXES)
    ny, nx, nz, nc = sizes
    devices = ny * nx * nz * nc
    scale = 1.0 / math.sqrt(HEAD)
    core_at = lax.axis_index("c")
    core = core_at.astype(jnp.int32)[None]
    place = lax.axis_index("x").astype(jnp.int32)[None]
    even = core_at == 0
    core, place, even, query_rows = lax.optimization_barrier((core, place, even, query_rows))

    def both_halves(mine, other):
        return jnp.where(
            even, jnp.concatenate([mine, other], 1), jnp.concatenate([other, mine], 1)
        )

    mine, other = pack(core, query_rows, key_rows, value_rows, out_grad)
    part = to_chip(other, devices, 0, 1)
    key, value, query, grad = join(mine, part)
    keys = (to_chip(key, devices, 1, 0), key, to_chip(key, devices, -1, 0))
    values = (to_chip(value, devices, 1, 0), value, to_chip(value, devices, -1, 0))

    inputs, _ = lax.optimization_barrier((inputs, key))
    blocks = input_blocks(place, inputs, to_chip(inputs, devices, 0, 1), nx, ny)

    blocks, query = lax.optimization_barrier((blocks, query))
    taken = [blocks[0]] + [along_x(blocks[step], sizes, step) for step in range(1, nx)]

    prev, own, after, lse = value_pass(core, query, grad, keys, scale)
    from_next = to_chip(prev, devices, -1, 0)
    from_prev = to_chip(after, devices, 1, 0)
    dq, dq_other, key_prev, key_own, key_after = score_pass(
        core, query, grad, keys, values, lse, scale
    )
    from_next, from_prev, dq, key_prev, key_after = lax.optimization_barrier(
        (from_next, from_prev, dq, key_prev, key_after)
    )
    value_half = (own + from_next.astype(jnp.float32) + from_prev.astype(jnp.float32)).astype(
        jnp.bfloat16
    )
    gathered = [value_half] + [along_x(value_half, sizes, step) for step in range(1, nx)]
    key_from_next = to_chip(key_prev, devices, -1, 0)
    key_from_prev = to_chip(key_after, devices, 1, 0)
    value_back = to_chip(value_half[rows:], devices, 0, 1)
    query_back = to_chip(dq_other, devices, 0, 1)

    partial = weight_pass(taken, gathered)
    half = features // 2
    own_count = inputs.shape[1] // devices
    pieces = partial.reshape(ny * nz * nc, own_count, half)
    arrived = lax.all_to_all(pieces, ("y", "z", "c"), 0, 0, tiled=True)
    summed = jnp.sum(
        arrived.reshape(ny * nz, nc, own_count, half).astype(jnp.float32), axis=0
    )
    weight_grad = summed.transpose(1, 0, 2).reshape(own_count, features) * (
        1.0 / math.sqrt(rows * devices)
    )

    key_half = (
        key_own + key_from_next.astype(jnp.float32) + key_from_prev.astype(jnp.float32)
    ).astype(jnp.bfloat16)
    key_back = to_chip(key_half[rows:], devices, 0, 1)
    query_grad = both_halves(dq, query_back)
    value_grad = both_halves(value_half[:rows], value_back)
    key_grad = both_halves(key_half[:rows], key_back)
    return (query_grad, key_grad, value_grad, weight_grad)


def solution(mesh):
    fine = physical_mesh(mesh)
    spec = P(AXES, None)
    return jax.shard_map(
        local,
        mesh=fine,
        in_specs=(spec,) * 5,
        out_specs=(spec,) * 4,
        check_vma=False,
    )
```

```python
import math

import jax
import jax.numpy as jnp
from jax import lax
from jax.experimental import pallas as pl
from jax.experimental.pallas import tpu as pltpu
from jax.sharding import Mesh, PartitionSpec as P


HEAD = 128
NEG = -1e30
ROOM = pltpu.CompilerParams(vmem_limit_bytes=20 << 20)


AXES = ("y", "x", "z", "c")
LAST = (((1,), (1,)), ((), ()))
FIRST = (((0,), (0,)), ((), ()))


def physical_mesh(mesh):
    count = mesh.devices.size
    sizes = (4, 4, 8, 2) if count == 256 else (2, count // 8, 2, 2)
    return Mesh(mesh.devices.reshape(sizes), AXES)


def to_core(array, count):
    return lax.ppermute(array, AXES, [(device, device ^ 1) for device in range(count)])


def swap(array, count, odd):
    chips = count // 2
    pairs = []
    for device in range(count):
        chip, core = device // 2, device % 2
        other = ((chip - odd) ^ 1) + odd
        pairs.append((device, other % chips * 2 + core))
    return lax.ppermute(array, AXES, pairs)


def along_x(array, sizes, step):
    ny, nx, nz, nc = sizes
    pairs = []
    for y in range(ny):
        for x in range(nx):
            for rest in range(nz * nc):
                pairs.append(
                    ((y * nx + x) * nz * nc + rest, (y * nx + (x + step) % nx) * nz * nc + rest)
                )
    return lax.ppermute(array, AXES, pairs)


def vmem(count):
    return [pl.BlockSpec(memory_space=pltpu.VMEM)] * count


def smem():
    return pl.BlockSpec(memory_space=pltpu.SMEM)


def pack_kernel(core, query, key, value, grad, mine, other, done):
    half = query.shape[1] // 2
    here = pl.multiple_of(core[0] * half, half)
    there = pl.multiple_of((1 - core[0]) * half, half)
    copies = []
    for at, source in enumerate((key, query, grad, value)):
        for side, (target, start) in enumerate(((other, there), (mine, here))):
            copies.append(
                pltpu.make_async_copy(
                    source.at[:, pl.ds(start, half)], target.at[at], done.at[2 * at + side]
                )
            )
    for copy in copies:
        copy.start()
    for copy in copies:
        copy.wait()


def pack(core, query, key, value, grad):
    rows, features = query.shape
    four = jax.ShapeDtypeStruct((4, rows, features // 2), query.dtype)
    return pl.pallas_call(
        pack_kernel,
        out_shape=(four, four),
        in_specs=[smem()] + [pl.BlockSpec(memory_space=pltpu.HBM)] * 4,
        out_specs=tuple(vmem(2)),
        scratch_shapes=[pltpu.SemaphoreType.DMA((8,))],
        compiler_params=ROOM,
        name="pack",
    )(core, query, key, value, grad)


def join_kernel(mine, part, key, query, grad, value):
    rows = mine.shape[1]
    for at, target in enumerate((key, query, grad, value)):
        target[:rows] = mine[at]
        target[rows:] = part[at]


def join(mine, part):
    _, rows, half = mine.shape
    two = jax.ShapeDtypeStruct((2 * rows, half), mine.dtype)
    return pl.pallas_call(
        join_kernel,
        out_shape=(two,) * 4,
        in_specs=vmem(2),
        out_specs=tuple(vmem(4)),
        compiler_params=ROOM,
        name="join",
    )(mine, part)


def window_bias(place, tokens):
    even_core, even_chip = place[0] == 0, place[1] == 0
    left = lax.broadcasted_iota(jnp.int32, (1, 2 * tokens), 1) < tokens
    right = jnp.logical_not(left)

    def bias(core_even, chip_even, columns):
        hit = jnp.logical_and(even_core == core_even, even_chip == chip_even)
        return jnp.where(jnp.logical_and(hit, columns), NEG, 0.0)

    return {
        0: bias(True, False, right) + bias(False, True, right),
        1: bias(True, True, left) + bias(False, False, left),
        4: bias(True, True, right) + bias(False, False, right),
        5: bias(True, False, left) + bias(False, True, left),
    }


def scores_of(bias, keys, queries, scale):
    flat = lax.dot_general(keys, queries, LAST, preferred_element_type=jnp.float32) * scale
    size = flat.shape[0] // 6
    parts = []
    for block in range(6):
        part = flat[block * size : (block + 1) * size]
        parts.append(part + bias[block] if block in bias else part)
    return jnp.concatenate(parts, 0)


def value_kernel(scale, place, query, grad, first_k, key, second_k, first, own, second, lse):
    two, width = query.shape
    bias = window_bias(place, two // 2)
    for head in range(width // HEAD):
        at = slice(head * HEAD, (head + 1) * HEAD)
        keys = jnp.concatenate([first_k[:, at], key[:, at], second_k[:, at]], 0)
        scores = scores_of(bias, keys, query[:, at], scale)
        top = jnp.max(scores, axis=0, keepdims=True)
        raised = jnp.exp(scores - top)
        total = jnp.sum(raised, axis=0, keepdims=True)
        probs = (raised * (1.0 / total)).astype(jnp.bfloat16)
        terms = jnp.dot(probs, grad[:, at], preferred_element_type=jnp.float32)
        first[:, at] = terms[:two].astype(jnp.bfloat16)
        own[:, at] = terms[two : 2 * two]
        second[:, at] = terms[2 * two :].astype(jnp.bfloat16)
        lse[head] = jnp.broadcast_to(top + jnp.log(total), lse.shape[1:])


def score_kernel(
    scale, place, query, grad, first_k, key, second_k, first_v, value, second_v, lse,
    query_grad, query_back, first, own, second,
):
    two, width = query.shape
    bias = window_bias(place, two // 2)
    for head in range(width // HEAD):
        at = slice(head * HEAD, (head + 1) * HEAD)
        keys = jnp.concatenate([first_k[:, at], key[:, at], second_k[:, at]], 0)
        values = jnp.concatenate([first_v[:, at], value[:, at], second_v[:, at]], 0)
        scores = scores_of(bias, keys, query[:, at], scale)
        probs = jnp.exp(scores - lse[head, 0:1])
        grad_probs = lax.dot_general(values, grad[:, at], LAST, preferred_element_type=jnp.float32)
        rounded = probs.astype(jnp.bfloat16).astype(jnp.float32)
        delta = jnp.sum(rounded * grad_probs, axis=0, keepdims=True)
        low = (probs * (grad_probs - delta)).astype(jnp.bfloat16)
        turned = lax.dot_general(keys, low, FIRST, preferred_element_type=jnp.float32) * scale
        found = turned.T.astype(jnp.bfloat16)
        query_grad[:, at] = found[: two // 2]
        query_back[:, at] = found[two // 2 :]
        terms = jnp.dot(low, query[:, at], preferred_element_type=jnp.float32) * scale
        first[:, at] = terms[:two].astype(jnp.bfloat16)
        own[:, at] = terms[two : 2 * two]
        second[:, at] = terms[2 * two :].astype(jnp.bfloat16)


def value_pass(core, query, grad, keys, scale):
    two, width = query.shape
    heads = width // HEAD
    low = jax.ShapeDtypeStruct((two, width), jnp.bfloat16)
    high = jax.ShapeDtypeStruct((two, width), jnp.float32)
    work = heads * two * 3 * two
    return pl.pallas_call(
        lambda *refs: value_kernel(scale, *refs),
        out_shape=(low, high, low, jax.ShapeDtypeStruct((heads, 8, two), jnp.float32)),
        in_specs=[smem()] + vmem(5),
        out_specs=tuple(vmem(4)),
        cost_estimate=pl.CostEstimate(
            flops=4 * work * HEAD, transcendentals=work, bytes_accessed=4 << 20
        ),
        compiler_params=ROOM,
        name="value_pass",
    )(core, query, grad, *keys)


def score_pass(core, query, grad, keys, values, lse, scale):
    two, width = query.shape
    heads = width // HEAD
    low = jax.ShapeDtypeStruct((two, width), jnp.bfloat16)
    high = jax.ShapeDtypeStruct((two, width), jnp.float32)
    part = jax.ShapeDtypeStruct((two // 2, width), jnp.bfloat16)
    work = heads * two * 3 * two
    return pl.pallas_call(
        lambda *refs: score_kernel(scale, *refs),
        out_shape=(part, part, low, high, low),
        in_specs=[smem()] + vmem(9),
        out_specs=tuple(vmem(5)),
        cost_estimate=pl.CostEstimate(
            flops=8 * work * HEAD, transcendentals=work, bytes_accessed=6 << 20
        ),
        compiler_params=ROOM,
        name="score_pass",
    )(core, query, grad, *keys, *values, lse)


def block_kernel(count, groups, place, own, part, *blocks):
    rows, width = own.shape
    size = width // (groups * count)
    for step, block in enumerate(blocks):
        target = lax.rem(place[2] + step, count)
        for group in range(groups):
            start = pl.multiple_of((group * count + target) * size, size)
            at = slice(group * size, (group + 1) * size)
            block[:rows, at] = own[:, pl.ds(start, size)]
            block[rows:, at] = part[:, pl.ds(start, size)]


def input_blocks(place, own, part, count, groups):
    rows, width = own.shape
    block = jax.ShapeDtypeStruct((2 * rows, width // count), own.dtype)
    return pl.pallas_call(
        lambda *refs: block_kernel(count, groups, *refs),
        out_shape=(block,) * count,
        in_specs=[smem()] + vmem(2),
        out_specs=tuple(vmem(count)),
        compiler_params=ROOM,
        name="input_blocks",
    )(place, own, part)


def weight_kernel(count, *refs):
    inputs, gathered, out = refs[:count], refs[count : 2 * count], refs[2 * count]
    tile = 256
    for low in range(0, out.shape[0], tile):
        total = jnp.zeros((tile, out.shape[1]), jnp.float32)
        for step in range(count):
            total += lax.dot_general(
                inputs[step][:, low : low + tile],
                gathered[step][...],
                FIRST,
                preferred_element_type=jnp.float32,
            )
        out[low : low + tile] = total.astype(jnp.bfloat16)


def weight_pass(inputs, gathered):
    count = len(inputs)
    rows, width = inputs[0].shape
    columns = gathered[0].shape[1]
    return pl.pallas_call(
        lambda *refs: weight_kernel(count, *refs),
        out_shape=jax.ShapeDtypeStruct((width, columns), jnp.bfloat16),
        in_specs=vmem(2 * count),
        out_specs=pl.BlockSpec(memory_space=pltpu.VMEM),
        cost_estimate=pl.CostEstimate(
            flops=2 * count * rows * width * columns, transcendentals=0, bytes_accessed=4 << 20
        ),
        compiler_params=ROOM,
        name="weight_pass",
    )(*inputs, *gathered)


def steps(query_rows, key_rows, value_rows, out_grad, inputs):
    rows, features = query_rows.shape
    sizes = tuple(lax.axis_size(name) for name in AXES)
    ny, nx, nz, nc = sizes
    devices = ny * nx * nz * nc
    scale = 1.0 / math.sqrt(HEAD)
    core = lax.axis_index("c").astype(jnp.int32)
    parity = lax.rem(lax.axis_index("z").astype(jnp.int32), 2)
    place = jnp.stack([core, parity, lax.axis_index("x").astype(jnp.int32)])
    even = core == 0
    place, even, query_rows = lax.optimization_barrier((place, even, query_rows))

    def both_halves(mine, other):
        return jnp.where(
            even, jnp.concatenate([mine, other], 1), jnp.concatenate([other, mine], 1)
        )

    def swaps(one, two):
        got_one = swap(one, devices, 0)
        got_two = swap(two, devices, 1)
        return got_one, got_two

    mine, other = pack(place, query_rows, key_rows, value_rows, out_grad)
    part = to_core(other, devices)
    key, query, grad, value = join(mine, part)
    first_k, second_k = swaps(key, key)
    first_v, second_v = swaps(value, value)
    keys, values = (first_k, key, second_k), (first_v, value, second_v)

    inputs, _ = lax.optimization_barrier((inputs, mine))
    inputs_part = to_core(inputs, devices)
    blocks = input_blocks(place, inputs, inputs_part, nx, ny)
    taken = [blocks[0]]
    for step in range(1, nx):
        taken.append(along_x(blocks[step], sizes, step))

    first, own, second, lse = value_pass(place, query, grad, keys, scale)
    from_first, from_second = swaps(first, second)
    dq, dq_other, key_first, key_own, key_second = score_pass(
        place, query, grad, keys, values, lse, scale
    )
    from_first, from_second, dq, key_first, key_second = lax.optimization_barrier(
        (from_first, from_second, dq, key_first, key_second)
    )
    value_half = (own + from_first.astype(jnp.float32) + from_second.astype(jnp.float32)).astype(
        jnp.bfloat16
    )
    gathered = [value_half]
    for step in range(1, nx):
        gathered.append(along_x(value_half, sizes, step))
    key_from_first, key_from_second = swaps(key_first, key_second)
    value_back = to_core(value_half[rows:], devices)
    query_back = to_core(dq_other, devices)

    partial = weight_pass(taken, gathered)
    half = features // 2
    own_count = inputs.shape[1] // devices
    pieces = partial.reshape(ny * nz * nc, own_count, half)
    arrived = lax.all_to_all(pieces, ("y", "z", "c"), 0, 0, tiled=True)
    summed = jnp.sum(
        arrived.reshape(ny * nz, nc, own_count, half).astype(jnp.float32), axis=0
    )
    weight_grad = summed.transpose(1, 0, 2).reshape(own_count, features) * (
        1.0 / math.sqrt(rows * devices)
    )

    key_half = (
        key_own + key_from_first.astype(jnp.float32) + key_from_second.astype(jnp.float32)
    ).astype(jnp.bfloat16)
    key_back = to_core(key_half[rows:], devices)
    query_grad = both_halves(dq, query_back)
    value_grad = both_halves(value_half[:rows], value_back)
    key_grad = both_halves(key_half[:rows], key_back)
    return (query_grad, key_grad, value_grad, weight_grad)


def solution(mesh):
    fine = physical_mesh(mesh)
    spec = P(AXES, None)
    return jax.shard_map(
        steps,
        mesh=fine,
        in_specs=(spec,) * 5,
        out_specs=(spec,) * 4,
        check_vma=False,
    )
```

```python
import math

import jax
import jax.numpy as jnp
from jax import lax
from jax.experimental import pallas as pl
from jax.experimental.pallas import tpu as pltpu
from jax.sharding import Mesh, PartitionSpec as P


HEAD = 128
NEG = -1e30
ROOM = pltpu.CompilerParams(vmem_limit_bytes=20 << 20)


AXES = ("y", "x", "z", "c")
LAST = (((1,), (1,)), ((), ()))
FIRST = (((0,), (0,)), ((), ()))


def physical_mesh(mesh):
    count = mesh.devices.size
    sizes = (4, 4, 8, 2) if count == 256 else (2, count // 8, 2, 2)
    return Mesh(mesh.devices.reshape(sizes), AXES)


def to_core(array, count):
    return lax.ppermute(array, AXES, [(device, device ^ 1) for device in range(count)])


def swap(array, count, odd):
    chips = count // 2
    pairs = []
    for device in range(count):
        chip, core = device // 2, device % 2
        other = ((chip - odd) ^ 1) + odd
        pairs.append((device, other % chips * 2 + core))
    return lax.ppermute(array, AXES, pairs)


def along_y(array, sizes, step):
    ny, nx, nz, nc = sizes
    rest = nx * nz * nc
    pairs = [(device, (device + step * rest) % (ny * rest)) for device in range(ny * rest)]
    return lax.ppermute(array, AXES, pairs)


def vmem(count):
    return [pl.BlockSpec(memory_space=pltpu.VMEM)] * count


def smem():
    return pl.BlockSpec(memory_space=pltpu.SMEM)


def pack_kernel(core, query, key, value, grad, mine, other, done):
    half = query.shape[1] // 2
    here = pl.multiple_of(core[0] * half, half)
    there = pl.multiple_of((1 - core[0]) * half, half)
    copies = []
    for at, source in enumerate((key, query, grad, value)):
        for side, (target, start) in enumerate(((other, there), (mine, here))):
            copies.append(
                pltpu.make_async_copy(
                    source.at[:, pl.ds(start, half)], target.at[at], done.at[2 * at + side]
                )
            )
    for copy in copies:
        copy.start()
    for copy in copies:
        copy.wait()


def pack(core, query, key, value, grad):
    rows, features = query.shape
    four = jax.ShapeDtypeStruct((4, rows, features // 2), query.dtype)
    return pl.pallas_call(
        pack_kernel,
        out_shape=(four, four),
        in_specs=[smem()] + [pl.BlockSpec(memory_space=pltpu.HBM)] * 4,
        out_specs=tuple(vmem(2)),
        scratch_shapes=[pltpu.SemaphoreType.DMA((8,))],
        compiler_params=ROOM,
        name="pack",
    )(core, query, key, value, grad)


def join_kernel(mine, part, key, query, grad, value):
    rows = mine.shape[1]
    for at, target in enumerate((key, query, grad, value)):
        target[:rows] = mine[at]
        target[rows:] = part[at]


def join(mine, part):
    _, rows, half = mine.shape
    two = jax.ShapeDtypeStruct((2 * rows, half), mine.dtype)
    return pl.pallas_call(
        join_kernel,
        out_shape=(two,) * 4,
        in_specs=vmem(2),
        out_specs=tuple(vmem(4)),
        compiler_params=ROOM,
        name="join",
    )(mine, part)


def window_bias(place, tokens):
    even_core, even_chip = place[0] == 0, place[1] == 0
    left = lax.broadcasted_iota(jnp.int32, (1, 2 * tokens), 1) < tokens
    right = jnp.logical_not(left)

    def bias(core_even, chip_even, columns):
        hit = jnp.logical_and(even_core == core_even, even_chip == chip_even)
        return jnp.where(jnp.logical_and(hit, columns), NEG, 0.0)

    return {
        0: bias(True, False, right) + bias(False, True, right),
        1: bias(True, True, left) + bias(False, False, left),
        4: bias(True, True, right) + bias(False, False, right),
        5: bias(True, False, left) + bias(False, True, left),
    }


def scores_of(bias, keys, queries, scale):
    flat = lax.dot_general(keys, queries, LAST, preferred_element_type=jnp.float32) * scale
    size = flat.shape[0] // 6
    parts = []
    for block in range(6):
        part = flat[block * size : (block + 1) * size]
        parts.append(part + bias[block] if block in bias else part)
    return jnp.concatenate(parts, 0)


def value_kernel(scale, place, query, grad, first_k, key, second_k, first, own, second, lse):
    two, width = query.shape
    bias = window_bias(place, two // 2)
    for head in range(width // HEAD):
        at = slice(head * HEAD, (head + 1) * HEAD)
        keys = jnp.concatenate([first_k[:, at], key[:, at], second_k[:, at]], 0)
        scores = scores_of(bias, keys, query[:, at], scale)
        top = jnp.max(scores, axis=0, keepdims=True)
        raised = jnp.exp(scores - top)
        total = jnp.sum(raised, axis=0, keepdims=True)
        probs = (raised * (1.0 / total)).astype(jnp.bfloat16)
        terms = jnp.dot(probs, grad[:, at], preferred_element_type=jnp.float32)
        first[:, at] = terms[:two].astype(jnp.bfloat16)
        own[:, at] = terms[two : 2 * two]
        second[:, at] = terms[2 * two :].astype(jnp.bfloat16)
        lse[head] = jnp.broadcast_to(top + jnp.log(total), lse.shape[1:])


def score_kernel(
    scale, place, query, grad, first_k, key, second_k, first_v, value, second_v, lse,
    query_grad, query_back, first, own, second,
):
    two, width = query.shape
    bias = window_bias(place, two // 2)
    for head in range(width // HEAD):
        at = slice(head * HEAD, (head + 1) * HEAD)
        keys = jnp.concatenate([first_k[:, at], key[:, at], second_k[:, at]], 0)
        values = jnp.concatenate([first_v[:, at], value[:, at], second_v[:, at]], 0)
        scores = scores_of(bias, keys, query[:, at], scale)
        probs = jnp.exp(scores - lse[head, 0:1])
        grad_probs = lax.dot_general(values, grad[:, at], LAST, preferred_element_type=jnp.float32)
        rounded = probs.astype(jnp.bfloat16).astype(jnp.float32)
        delta = jnp.sum(rounded * grad_probs, axis=0, keepdims=True)
        low = (probs * (grad_probs - delta)).astype(jnp.bfloat16)
        turned = lax.dot_general(keys, low, FIRST, preferred_element_type=jnp.float32) * scale
        found = turned.T.astype(jnp.bfloat16)
        query_grad[:, at] = found[: two // 2]
        query_back[:, at] = found[two // 2 :]
        terms = jnp.dot(low, query[:, at], preferred_element_type=jnp.float32) * scale
        first[:, at] = terms[:two].astype(jnp.bfloat16)
        own[:, at] = terms[two : 2 * two]
        second[:, at] = terms[2 * two :].astype(jnp.bfloat16)


def value_pass(core, query, grad, keys, scale):
    two, width = query.shape
    heads = width // HEAD
    low = jax.ShapeDtypeStruct((two, width), jnp.bfloat16)
    high = jax.ShapeDtypeStruct((two, width), jnp.float32)
    work = heads * two * 3 * two
    return pl.pallas_call(
        lambda *refs: value_kernel(scale, *refs),
        out_shape=(low, high, low, jax.ShapeDtypeStruct((heads, 8, two), jnp.float32)),
        in_specs=[smem()] + vmem(5),
        out_specs=tuple(vmem(4)),
        cost_estimate=pl.CostEstimate(
            flops=4 * work * HEAD, transcendentals=work, bytes_accessed=4 << 20
        ),
        compiler_params=ROOM,
        name="value_pass",
    )(core, query, grad, *keys)


def score_pass(core, query, grad, keys, values, lse, scale):
    two, width = query.shape
    heads = width // HEAD
    low = jax.ShapeDtypeStruct((two, width), jnp.bfloat16)
    high = jax.ShapeDtypeStruct((two, width), jnp.float32)
    part = jax.ShapeDtypeStruct((two // 2, width), jnp.bfloat16)
    work = heads * two * 3 * two
    return pl.pallas_call(
        lambda *refs: score_kernel(scale, *refs),
        out_shape=(part, part, low, high, low),
        in_specs=[smem()] + vmem(9),
        out_specs=tuple(vmem(5)),
        cost_estimate=pl.CostEstimate(
            flops=8 * work * HEAD, transcendentals=work, bytes_accessed=6 << 20
        ),
        compiler_params=ROOM,
        name="score_pass",
    )(core, query, grad, *keys, *values, lse)


def block_kernel(count, place, own, *blocks):
    size = own.shape[1] // count
    for step, block in enumerate(blocks):
        target = lax.rem(place[2] + step, count)
        block[...] = own[:, pl.ds(pl.multiple_of(target * size, size), size)]


def input_blocks(place, own, count):
    rows, width = own.shape
    block = jax.ShapeDtypeStruct((rows, width // count), own.dtype)
    return pl.pallas_call(
        lambda *refs: block_kernel(count, *refs),
        out_shape=(block,) * count,
        in_specs=[smem()] + vmem(1),
        out_specs=tuple(vmem(count)),
        compiler_params=ROOM,
        name="input_blocks",
    )(place, own)


def stack_kernel(count, *refs):
    for step in range(count):
        refs[count][step] = refs[step][...]


def stack(blocks):
    count = len(blocks)
    return pl.pallas_call(
        lambda *refs: stack_kernel(count, *refs),
        out_shape=jax.ShapeDtypeStruct((count,) + blocks[0].shape, blocks[0].dtype),
        in_specs=vmem(count),
        out_specs=pl.BlockSpec(memory_space=pltpu.VMEM),
        compiler_params=ROOM,
        name="stack",
    )(*blocks)


def weight_kernel(count, own, part, *refs):
    gathered, out = refs[:count], refs[count]
    rows = own.shape[1]
    tile = 256
    for low in range(0, out.shape[0], tile):
        total = jnp.zeros((tile, out.shape[1]), jnp.float32)
        for step in range(count):
            for held, start in ((own, 0), (part, rows)):
                total += lax.dot_general(
                    held[step, :, low : low + tile],
                    gathered[step][start : start + rows],
                    FIRST,
                    preferred_element_type=jnp.float32,
                )
        out[low : low + tile] = total.astype(jnp.bfloat16)


def weight_pass(own, part, gathered):
    count, rows, width = own.shape
    columns = gathered[0].shape[1]
    return pl.pallas_call(
        lambda *refs: weight_kernel(count, *refs),
        out_shape=jax.ShapeDtypeStruct((width, columns), jnp.bfloat16),
        in_specs=vmem(2 + count),
        out_specs=pl.BlockSpec(memory_space=pltpu.VMEM),
        cost_estimate=pl.CostEstimate(
            flops=4 * count * rows * width * columns, transcendentals=0, bytes_accessed=4 << 20
        ),
        compiler_params=ROOM,
        name="weight_pass",
    )(own, part, *gathered)


def steps(query_rows, key_rows, value_rows, out_grad, inputs):
    rows, features = query_rows.shape
    sizes = tuple(lax.axis_size(name) for name in AXES)
    ny, nx, nz, nc = sizes
    devices = ny * nx * nz * nc
    scale = 1.0 / math.sqrt(HEAD)
    core = lax.axis_index("c").astype(jnp.int32)
    parity = lax.rem(lax.axis_index("z").astype(jnp.int32), 2)
    place = jnp.stack([core, parity, lax.axis_index("y").astype(jnp.int32)])
    even = core == 0
    place, even, query_rows = lax.optimization_barrier((place, even, query_rows))

    def both_halves(mine, other):
        return jnp.where(
            even, jnp.concatenate([mine, other], 1), jnp.concatenate([other, mine], 1)
        )

    def swaps(one, two):
        got_one = swap(one, devices, 0)
        got_two = swap(two, devices, 1)
        return got_one, got_two

    mine, other = pack(place, query_rows, key_rows, value_rows, out_grad)
    part = to_core(other, devices)
    key, query, grad, value = join(mine, part)
    first_k, second_k = swaps(key, key)
    first_v, second_v = swaps(value, value)
    keys, values = (first_k, key, second_k), (first_v, value, second_v)

    inputs, _ = lax.optimization_barrier((inputs, mine))
    blocks = input_blocks(place, inputs, ny)
    taken = [blocks[0]]
    for step in range(1, ny):
        taken.append(along_y(blocks[step], sizes, step))
    taken = stack(taken)
    taken_part = to_core(taken, devices)

    first, own, second, lse = value_pass(place, query, grad, keys, scale)
    from_first, from_second = swaps(first, second)
    dq, dq_other, key_first, key_own, key_second = score_pass(
        place, query, grad, keys, values, lse, scale
    )
    from_first, from_second, dq, key_first, key_second = lax.optimization_barrier(
        (from_first, from_second, dq, key_first, key_second)
    )
    value_half = (own + from_first.astype(jnp.float32) + from_second.astype(jnp.float32)).astype(
        jnp.bfloat16
    )
    gathered = [value_half]
    for step in range(1, ny):
        gathered.append(along_y(value_half, sizes, step))
    key_from_first, key_from_second = swaps(key_first, key_second)
    value_back = to_core(value_half[rows:], devices)
    query_back = to_core(dq_other, devices)

    partial = weight_pass(taken, taken_part, gathered)
    half = features // 2
    own_count = inputs.shape[1] // devices
    pieces = partial.reshape(nx * nz * nc, own_count, half)
    arrived = lax.all_to_all(pieces, ("x", "z", "c"), 0, 0, tiled=True)
    summed = jnp.sum(
        arrived.reshape(nx * nz, nc, own_count, half).astype(jnp.float32), axis=0
    )
    weight_grad = summed.transpose(1, 0, 2).reshape(own_count, features) * (
        1.0 / math.sqrt(rows * devices)
    )

    key_half = (
        key_own + key_from_first.astype(jnp.float32) + key_from_second.astype(jnp.float32)
    ).astype(jnp.bfloat16)
    key_back = to_core(key_half[rows:], devices)
    query_grad = both_halves(dq, query_back)
    value_grad = both_halves(value_half[:rows], value_back)
    key_grad = both_halves(key_half[:rows], key_back)
    return (query_grad, key_grad, value_grad, weight_grad)


def solution(mesh):
    fine = physical_mesh(mesh)
    spec = P(AXES, None)
    return jax.shard_map(
        steps,
        mesh=fine,
        in_specs=(spec,) * 5,
        out_specs=(spec,) * 4,
        check_vma=False,
    )
```

```python
import math

import jax
import jax.numpy as jnp
from jax import lax
from jax.experimental import pallas as pl
from jax.experimental.pallas import tpu as pltpu
from jax.sharding import Mesh, PartitionSpec as P


HEAD = 128
NEG = -1e30
ROOM = pltpu.CompilerParams(vmem_limit_bytes=20 << 20)


AXES = ("y", "x", "z", "c")
LAST = (((1,), (1,)), ((), ()))
FIRST = (((0,), (0,)), ((), ()))


def physical_mesh(mesh):
    count = mesh.devices.size
    sizes = (4, 4, 8, 2) if count == 256 else (2, count // 8, 2, 2)
    return Mesh(mesh.devices.reshape(sizes), AXES)


def to_core(array, count):
    return lax.ppermute(array, AXES, [(device, device ^ 1) for device in range(count)])


def swap(array, count, odd):
    chips = count // 2
    pairs = []
    for device in range(count):
        chip, core = device // 2, device % 2
        other = ((chip - odd) ^ 1) + odd
        pairs.append((device, other % chips * 2 + core))
    return lax.ppermute(array, AXES, pairs)


def along_y(array, sizes, step):
    ny, nx, nz, nc = sizes
    rest = nx * nz * nc
    pairs = [(device, (device + step * rest) % (ny * rest)) for device in range(ny * rest)]
    return lax.ppermute(array, AXES, pairs)


def vmem(count):
    return [pl.BlockSpec(memory_space=pltpu.VMEM)] * count


def smem():
    return pl.BlockSpec(memory_space=pltpu.SMEM)


def pack_kernel(core, key, query, grad, value, key_mine, key_other, mine, other, done):
    half = query.shape[1] // 2
    here = pl.multiple_of(core[0] * half, half)
    there = pl.multiple_of((1 - core[0]) * half, half)
    moves = [(key, key_other, there), (key, key_mine, here)]
    for at, source in enumerate((query, grad, value)):
        moves += [(source, other.at[at], there), (source, mine.at[at], here)]
    copies = [
        pltpu.make_async_copy(source.at[:, pl.ds(start, half)], target, done.at[at])
        for at, (source, target, start) in enumerate(moves)
    ]
    for copy in copies:
        copy.start()
    for copy in copies:
        copy.wait()


def pack(core, key, query, grad, value):
    rows, features = query.shape
    one = jax.ShapeDtypeStruct((rows, features // 2), query.dtype)
    three = jax.ShapeDtypeStruct((3, rows, features // 2), query.dtype)
    return pl.pallas_call(
        pack_kernel,
        out_shape=(one, one, three, three),
        in_specs=[smem()] + [pl.BlockSpec(memory_space=pltpu.HBM)] * 4,
        out_specs=tuple(vmem(4)),
        scratch_shapes=[pltpu.SemaphoreType.DMA((8,))],
        compiler_params=ROOM,
        name="pack",
    )(core, *(in_hbm(array) for array in (key, query, grad, value)))


def in_hbm(array):
    return pltpu.with_memory_space_constraint(array, pltpu.HBM)


def join_kernel(count, mine, part, *targets):
    rows = mine.shape[-2]
    for at, target in enumerate(targets):
        target[:rows] = mine[at] if count > 1 else mine[...]
        target[rows:] = part[at] if count > 1 else part[...]


def join(mine, part, count):
    rows, half = mine.shape[-2:]
    two = jax.ShapeDtypeStruct((2 * rows, half), mine.dtype)
    return pl.pallas_call(
        lambda *refs: join_kernel(count, *refs),
        out_shape=(two,) * count,
        in_specs=vmem(2),
        out_specs=tuple(vmem(count)),
        compiler_params=ROOM,
        name="join",
    )(mine, part)


def window_bias(place, tokens):
    even_core, even_chip = place[0] == 0, place[1] == 0
    left = lax.broadcasted_iota(jnp.int32, (1, 2 * tokens), 1) < tokens
    right = jnp.logical_not(left)

    def bias(core_even, chip_even, columns):
        hit = jnp.logical_and(even_core == core_even, even_chip == chip_even)
        return jnp.where(jnp.logical_and(hit, columns), NEG, 0.0)

    return {
        0: bias(True, False, right) + bias(False, True, right),
        1: bias(True, True, left) + bias(False, False, left),
        4: bias(True, True, right) + bias(False, False, right),
        5: bias(True, False, left) + bias(False, True, left),
    }


def scores_of(bias, keys, queries, scale):
    flat = lax.dot_general(keys, queries, LAST, preferred_element_type=jnp.float32) * scale
    size = flat.shape[0] // 6
    parts = []
    for block in range(6):
        part = flat[block * size : (block + 1) * size]
        parts.append(part + bias[block] if block in bias else part)
    return jnp.concatenate(parts, 0)


def value_kernel(scale, place, query, grad, first_k, key, second_k, first, own, second, lse):
    two, width = query.shape
    bias = window_bias(place, two // 2)
    for head in range(width // HEAD):
        at = slice(head * HEAD, (head + 1) * HEAD)
        keys = jnp.concatenate([first_k[:, at], key[:, at], second_k[:, at]], 0)
        scores = scores_of(bias, keys, query[:, at], scale)
        top = jnp.max(scores, axis=0, keepdims=True)
        raised = jnp.exp(scores - top)
        total = jnp.sum(raised, axis=0, keepdims=True)
        probs = (raised * (1.0 / total)).astype(jnp.bfloat16)
        terms = jnp.dot(probs, grad[:, at], preferred_element_type=jnp.float32)
        first[:, at] = terms[:two].astype(jnp.bfloat16)
        own[:, at] = terms[two : 2 * two]
        second[:, at] = terms[2 * two :].astype(jnp.bfloat16)
        lse[head] = jnp.broadcast_to(top + jnp.log(total), lse.shape[1:])


def score_kernel(
    scale, place, query, grad, first_k, key, second_k, first_v, value, second_v, lse,
    query_grad, query_back, first, own, second,
):
    two, width = query.shape
    bias = window_bias(place, two // 2)
    for head in range(width // HEAD):
        at = slice(head * HEAD, (head + 1) * HEAD)
        keys = jnp.concatenate([first_k[:, at], key[:, at], second_k[:, at]], 0)
        values = jnp.concatenate([first_v[:, at], value[:, at], second_v[:, at]], 0)
        scores = scores_of(bias, keys, query[:, at], scale)
        probs = jnp.exp(scores - lse[head, 0:1])
        grad_probs = lax.dot_general(values, grad[:, at], LAST, preferred_element_type=jnp.float32)
        rounded = probs.astype(jnp.bfloat16).astype(jnp.float32)
        delta = jnp.sum(rounded * grad_probs, axis=0, keepdims=True)
        low = (probs * (grad_probs - delta)).astype(jnp.bfloat16)
        turned = lax.dot_general(keys, low, FIRST, preferred_element_type=jnp.float32) * scale
        found = turned.T.astype(jnp.bfloat16)
        query_grad[:, at] = found[: two // 2]
        query_back[:, at] = found[two // 2 :]
        terms = jnp.dot(low, query[:, at], preferred_element_type=jnp.float32) * scale
        first[:, at] = terms[:two].astype(jnp.bfloat16)
        own[:, at] = terms[two : 2 * two]
        second[:, at] = terms[2 * two :].astype(jnp.bfloat16)


def value_pass(core, query, grad, keys, scale):
    two, width = query.shape
    heads = width // HEAD
    low = jax.ShapeDtypeStruct((two, width), jnp.bfloat16)
    high = jax.ShapeDtypeStruct((two, width), jnp.float32)
    work = heads * two * 3 * two
    return pl.pallas_call(
        lambda *refs: value_kernel(scale, *refs),
        out_shape=(low, high, low, jax.ShapeDtypeStruct((heads, 8, two), jnp.float32)),
        in_specs=[smem()] + vmem(5),
        out_specs=tuple(vmem(4)),
        cost_estimate=pl.CostEstimate(
            flops=4 * work * HEAD, transcendentals=work, bytes_accessed=4 << 20
        ),
        compiler_params=ROOM,
        name="value_pass",
    )(core, query, grad, *keys)


def score_pass(core, query, grad, keys, values, lse, scale):
    two, width = query.shape
    heads = width // HEAD
    low = jax.ShapeDtypeStruct((two, width), jnp.bfloat16)
    high = jax.ShapeDtypeStruct((two, width), jnp.float32)
    part = jax.ShapeDtypeStruct((two // 2, width), jnp.bfloat16)
    work = heads * two * 3 * two
    return pl.pallas_call(
        lambda *refs: score_kernel(scale, *refs),
        out_shape=(part, part, low, high, low),
        in_specs=[smem()] + vmem(9),
        out_specs=tuple(vmem(5)),
        cost_estimate=pl.CostEstimate(
            flops=8 * work * HEAD, transcendentals=work, bytes_accessed=6 << 20
        ),
        compiler_params=ROOM,
        name="score_pass",
    )(core, query, grad, *keys, *values, lse)


def block_kernel(count, place, own, *blocks):
    size = own.shape[1] // count
    for step, block in enumerate(blocks):
        target = lax.rem(place[2] + step, count)
        block[...] = own[:, pl.ds(pl.multiple_of(target * size, size), size)]


def input_blocks(place, own, count):
    rows, width = own.shape
    block = jax.ShapeDtypeStruct((rows, width // count), own.dtype)
    return pl.pallas_call(
        lambda *refs: block_kernel(count, *refs),
        out_shape=(block,) * count,
        in_specs=[smem()] + vmem(1),
        out_specs=tuple(vmem(count)),
        compiler_params=ROOM,
        name="input_blocks",
    )(place, own)


def stack_kernel(count, *refs):
    for step in range(count):
        refs[count][step] = refs[step][...]


def stack(blocks):
    count = len(blocks)
    return pl.pallas_call(
        lambda *refs: stack_kernel(count, *refs),
        out_shape=jax.ShapeDtypeStruct((count,) + blocks[0].shape, blocks[0].dtype),
        in_specs=vmem(count),
        out_specs=pl.BlockSpec(memory_space=pltpu.VMEM),
        compiler_params=ROOM,
        name="stack",
    )(*blocks)


def weight_kernel(count, own, part, *refs):
    gathered, out = refs[:count], refs[count]
    rows = own.shape[1]
    tile = 256
    for low in range(0, out.shape[0], tile):
        total = jnp.zeros((tile, out.shape[1]), jnp.float32)
        for step in range(count):
            for held, start in ((own, 0), (part, rows)):
                total += lax.dot_general(
                    held[step, :, low : low + tile],
                    gathered[step][start : start + rows],
                    FIRST,
                    preferred_element_type=jnp.float32,
                )
        out[low : low + tile] = total.astype(jnp.bfloat16)


def weight_pass(own, part, gathered):
    count, rows, width = own.shape
    columns = gathered[0].shape[1]
    return pl.pallas_call(
        lambda *refs: weight_kernel(count, *refs),
        out_shape=jax.ShapeDtypeStruct((width, columns), jnp.bfloat16),
        in_specs=vmem(2 + count),
        out_specs=pl.BlockSpec(memory_space=pltpu.VMEM),
        cost_estimate=pl.CostEstimate(
            flops=4 * count * rows * width * columns, transcendentals=0, bytes_accessed=4 << 20
        ),
        compiler_params=ROOM,
        name="weight_pass",
    )(own, part, *gathered)


def steps(query_rows, key_rows, value_rows, out_grad, inputs):
    rows, features = query_rows.shape
    sizes = tuple(lax.axis_size(name) for name in AXES)
    ny, nx, nz, nc = sizes
    devices = ny * nx * nz * nc
    scale = 1.0 / math.sqrt(HEAD)
    core = lax.axis_index("c").astype(jnp.int32)
    parity = lax.rem(lax.axis_index("z").astype(jnp.int32), 2)
    place = jnp.stack([core, parity, lax.axis_index("y").astype(jnp.int32)])
    even = core == 0
    place, even, query_rows = lax.optimization_barrier((place, even, query_rows))

    def both_halves(mine, other):
        return jnp.where(
            even, jnp.concatenate([mine, other], 1), jnp.concatenate([other, mine], 1)
        )

    def swaps(one, two):
        got_one = swap(one, devices, 0)
        got_two = swap(two, devices, 1)
        return got_one, got_two

    key_mine, key_other, mine, other = pack(place, key_rows, query_rows, out_grad, value_rows)
    key_part = to_core(key_other, devices)
    part = to_core(other, devices)
    (key,) = join(key_mine, key_part, 1)
    first_k, second_k = swaps(key, key)
    keys = (first_k, key, second_k)
    query, grad, value = join(mine, part, 3)

    inputs, _ = lax.optimization_barrier((inputs, mine))
    blocks = input_blocks(place, inputs, ny)
    taken = [blocks[0]]
    for step in range(1, ny):
        taken.append(along_y(blocks[step], sizes, step))

    first, own, second, lse = value_pass(place, query, grad, keys, scale)
    from_first, from_second = swaps(first, second)
    value_half = (own + from_first.astype(jnp.float32) + from_second.astype(jnp.float32)).astype(
        jnp.bfloat16
    )
    first_v, second_v = swaps(value, value)
    query, _ = lax.optimization_barrier((query, value_half))
    dq, dq_other, key_first, key_own, key_second = score_pass(
        place, query, grad, keys, (first_v, value, second_v), lse, scale
    )
    *taken, _ = lax.optimization_barrier((*taken, value_half))
    taken = stack(taken)
    taken_part = to_core(taken, devices)
    gathered = [value_half]
    for step in range(1, ny):
        gathered.append(along_y(value_half, sizes, step))
    partial = weight_pass(taken, taken_part, gathered)
    key_from_first, key_from_second = swaps(key_first, key_second)
    value_back = to_core(value_half[rows:], devices)
    query_back = to_core(dq_other, devices)
    half = features // 2
    own_count = inputs.shape[1] // devices
    pieces = partial.reshape(nx * nz * nc, own_count, half)
    arrived = lax.all_to_all(pieces, ("x", "z", "c"), 0, 0, tiled=True)
    summed = jnp.sum(
        arrived.reshape(nx * nz, nc, own_count, half).astype(jnp.float32), axis=0
    )
    weight_grad = summed.transpose(1, 0, 2).reshape(own_count, features) * (
        1.0 / math.sqrt(rows * devices)
    )

    key_half = (
        key_own + key_from_first.astype(jnp.float32) + key_from_second.astype(jnp.float32)
    ).astype(jnp.bfloat16)
    key_back = to_core(key_half[rows:], devices)
    query_grad = both_halves(dq, query_back)
    value_grad = both_halves(value_half[:rows], value_back)
    key_grad = both_halves(key_half[:rows], key_back)
    return (query_grad, key_grad, value_grad, weight_grad)


def solution(mesh):
    fine = physical_mesh(mesh)
    spec = P(AXES, None)
    return jax.shard_map(
        steps,
        mesh=fine,
        in_specs=(spec,) * 5,
        out_specs=(spec,) * 4,
        check_vma=False,
    )
```

```python
import math

import jax
import jax.numpy as jnp
from jax import lax
from jax.experimental import pallas as pl
from jax.experimental.pallas import tpu as pltpu
from jax.sharding import Mesh, PartitionSpec as P


HEAD = 128
NEG = -1e30
ROOM = pltpu.CompilerParams(vmem_limit_bytes=20 << 20)


AXES = ("y", "x", "z", "c")
LAST = (((1,), (1,)), ((), ()))
FIRST = (((0,), (0,)), ((), ()))


def physical_mesh(mesh):
    count = mesh.devices.size
    sizes = (4, 4, 8, 2) if count == 256 else (2, count // 8, 2, 2)
    return Mesh(mesh.devices.reshape(sizes), AXES)


def to_core(array, count):
    return lax.ppermute(array, AXES, [(device, device ^ 1) for device in range(count)])


def swap(array, count, odd):
    chips = count // 2
    pairs = []
    for device in range(count):
        chip, core = device // 2, device % 2
        other = ((chip - odd) ^ 1) + odd
        pairs.append((device, other % chips * 2 + core))
    return lax.ppermute(array, AXES, pairs)


def along_y(array, sizes, step):
    ny, nx, nz, nc = sizes
    rest = nx * nz * nc
    pairs = [(device, (device + step * rest) % (ny * rest)) for device in range(ny * rest)]
    return lax.ppermute(array, AXES, pairs)


def vmem(count):
    return [pl.BlockSpec(memory_space=pltpu.VMEM)] * count


def smem():
    return pl.BlockSpec(memory_space=pltpu.SMEM)


def pack_kernel(core, key, query, grad, value, key_mine, key_other, mine, other, done):
    half = query.shape[1] // 2
    here = pl.multiple_of(core[0] * half, half)
    there = pl.multiple_of((1 - core[0]) * half, half)
    moves = [(key, key_other.at[0], there), (key, key_mine.at[0], here)]
    for at, source in enumerate((query, grad, value)):
        moves += [(source, other.at[at], there), (source, mine.at[at], here)]
    copies = [
        pltpu.make_async_copy(source.at[:, pl.ds(start, half)], target, done.at[at])
        for at, (source, target, start) in enumerate(moves)
    ]
    for copy in copies:
        copy.start()
    for copy in copies:
        copy.wait()


def pack(core, key, query, grad, value):
    rows, features = query.shape
    one, three = (
        jax.ShapeDtypeStruct((count, rows, features // 2), query.dtype) for count in (1, 3)
    )
    return pl.pallas_call(
        pack_kernel,
        out_shape=(one, one, three, three),
        in_specs=[smem()] + [pl.BlockSpec(memory_space=pltpu.HBM)] * 4,
        out_specs=tuple(vmem(4)),
        scratch_shapes=[pltpu.SemaphoreType.DMA((8,))],
        compiler_params=ROOM,
        name="pack",
    )(core, *(in_hbm(array) for array in (key, query, grad, value)))


def in_hbm(array):
    return pltpu.with_memory_space_constraint(array, pltpu.HBM)


def join_kernel(mine, part, *targets):
    rows = mine.shape[1]
    for at, target in enumerate(targets):
        target[:rows] = mine[at]
        target[rows:] = part[at]


def join(mine, part):
    count, rows, half = mine.shape
    two = jax.ShapeDtypeStruct((2 * rows, half), mine.dtype)
    return pl.pallas_call(
        join_kernel,
        out_shape=(two,) * count,
        in_specs=vmem(2),
        out_specs=tuple(vmem(count)),
        compiler_params=ROOM,
        name="join",
    )(mine, part)


def window_bias(place, tokens):
    left = lax.broadcasted_iota(jnp.int32, (1, 2 * tokens), 1) < tokens
    unlike = jnp.where(place[0] == place[1], 0.0, NEG)
    alike = jnp.where(place[0] == place[1], NEG, 0.0)
    return {
        0: jnp.where(left, 0.0, unlike),
        1: jnp.where(left, alike, 0.0),
        4: jnp.where(left, 0.0, alike),
        5: jnp.where(left, unlike, 0.0),
    }


def scores_of(bias, keys, queries, scale):
    flat = lax.dot_general(keys, queries, LAST, preferred_element_type=jnp.float32) * scale
    size = flat.shape[0] // 6
    parts = []
    for block in range(6):
        part = flat[block * size : (block + 1) * size]
        parts.append(part + bias[block] if block in bias else part)
    return jnp.concatenate(parts, 0)


def value_kernel(scale, place, query, grad, first_k, key, second_k, first, own, second, lse):
    two, width = query.shape
    bias = window_bias(place, two // 2)
    for head in range(width // HEAD):
        at = slice(head * HEAD, (head + 1) * HEAD)
        keys = jnp.concatenate([first_k[:, at], key[:, at], second_k[:, at]], 0)
        scores = scores_of(bias, keys, query[:, at], scale)
        top = jnp.max(scores, axis=0, keepdims=True)
        raised = jnp.exp(scores - top)
        total = jnp.sum(raised, axis=0, keepdims=True)
        probs = (raised * (1.0 / total)).astype(jnp.bfloat16)
        terms = jnp.dot(probs, grad[:, at], preferred_element_type=jnp.float32)
        first[:, at] = terms[:two].astype(jnp.bfloat16)
        own[:, at] = terms[two : 2 * two]
        second[:, at] = terms[2 * two :].astype(jnp.bfloat16)
        lse[head] = jnp.broadcast_to(top + jnp.log(total), lse.shape[1:])


def score_kernel(
    scale, place, query, grad, first_k, key, second_k, first_v, value, second_v, lse,
    query_grad, query_back, first, own, second,
):
    two, width = query.shape
    bias = window_bias(place, two // 2)
    for head in range(width // HEAD):
        at = slice(head * HEAD, (head + 1) * HEAD)
        keys = jnp.concatenate([first_k[:, at], key[:, at], second_k[:, at]], 0)
        values = jnp.concatenate([first_v[:, at], value[:, at], second_v[:, at]], 0)
        scores = scores_of(bias, keys, query[:, at], scale)
        probs = jnp.exp(scores - lse[head, 0:1])
        grad_probs = lax.dot_general(values, grad[:, at], LAST, preferred_element_type=jnp.float32)
        rounded = probs.astype(jnp.bfloat16).astype(jnp.float32)
        delta = jnp.sum(rounded * grad_probs, axis=0, keepdims=True)
        low = (probs * (grad_probs - delta)).astype(jnp.bfloat16)
        turned = lax.dot_general(keys, low, FIRST, preferred_element_type=jnp.float32) * scale
        found = turned.T.astype(jnp.bfloat16)
        query_grad[:, at] = found[: two // 2]
        query_back[:, at] = found[two // 2 :]
        terms = jnp.dot(low, query[:, at], preferred_element_type=jnp.float32) * scale
        first[:, at] = terms[:two].astype(jnp.bfloat16)
        own[:, at] = terms[two : 2 * two]
        second[:, at] = terms[2 * two :].astype(jnp.bfloat16)


def value_pass(core, query, grad, keys, scale):
    two, width = query.shape
    heads = width // HEAD
    low = jax.ShapeDtypeStruct((two, width), jnp.bfloat16)
    high = jax.ShapeDtypeStruct((two, width), jnp.float32)
    work = heads * two * 3 * two
    return pl.pallas_call(
        lambda *refs: value_kernel(scale, *refs),
        out_shape=(low, high, low, jax.ShapeDtypeStruct((heads, 8, two), jnp.float32)),
        in_specs=[smem()] + vmem(5),
        out_specs=tuple(vmem(4)),
        cost_estimate=pl.CostEstimate(
            flops=4 * work * HEAD, transcendentals=work, bytes_accessed=4 << 20
        ),
        compiler_params=ROOM,
        name="value_pass",
    )(core, query, grad, *keys)


def score_pass(core, query, grad, keys, values, lse, scale):
    two, width = query.shape
    heads = width // HEAD
    low = jax.ShapeDtypeStruct((two, width), jnp.bfloat16)
    high = jax.ShapeDtypeStruct((two, width), jnp.float32)
    part = jax.ShapeDtypeStruct((two // 2, width), jnp.bfloat16)
    work = heads * two * 3 * two
    return pl.pallas_call(
        lambda *refs: score_kernel(scale, *refs),
        out_shape=(part, part, low, high, low),
        in_specs=[smem()] + vmem(9),
        out_specs=tuple(vmem(5)),
        cost_estimate=pl.CostEstimate(
            flops=8 * work * HEAD, transcendentals=work, bytes_accessed=6 << 20
        ),
        compiler_params=ROOM,
        name="score_pass",
    )(core, query, grad, *keys, *values, lse)


def block_kernel(count, place, own, *blocks):
    size = own.shape[1] // count
    for step, block in enumerate(blocks):
        target = lax.rem(place[2] + step, count)
        block[...] = own[:, pl.ds(pl.multiple_of(target * size, size), size)]


def input_blocks(place, own, count):
    rows, width = own.shape
    block = jax.ShapeDtypeStruct((rows, width // count), own.dtype)
    return pl.pallas_call(
        lambda *refs: block_kernel(count, *refs),
        out_shape=(block,) * count,
        in_specs=[smem()] + vmem(1),
        out_specs=tuple(vmem(count)),
        compiler_params=ROOM,
        name="input_blocks",
    )(place, own)


def stack_kernel(count, *refs):
    for step in range(count):
        refs[count][step] = refs[step][...]


def stack(blocks):
    count = len(blocks)
    return pl.pallas_call(
        lambda *refs: stack_kernel(count, *refs),
        out_shape=jax.ShapeDtypeStruct((count,) + blocks[0].shape, blocks[0].dtype),
        in_specs=vmem(count),
        out_specs=pl.BlockSpec(memory_space=pltpu.VMEM),
        compiler_params=ROOM,
        name="stack",
    )(*blocks)


def merge_kernel(own, part, out):
    count, rows, _ = own.shape
    for step in range(count):
        at = 2 * step * rows
        out[:, at : at + rows] = own[step].T
        out[:, at + rows : at + 2 * rows] = part[step].T


def merge(own, part):
    count, rows, width = own.shape
    return pl.pallas_call(
        merge_kernel,
        out_shape=jax.ShapeDtypeStruct((width, 2 * count * rows), own.dtype),
        in_specs=vmem(2),
        out_specs=pl.BlockSpec(memory_space=pltpu.VMEM),
        compiler_params=ROOM,
        name="merge",
    )(own, part)


def weight_kernel(inputs, *refs):
    gathered, out = refs[:-1], refs[-1]
    rows = gathered[0].shape[0]
    tile = 256
    for low in range(0, out.shape[0], tile):
        total = jnp.zeros((tile, out.shape[1]), jnp.float32)
        for step, grads in enumerate(gathered):
            total += jnp.dot(
                inputs[low : low + tile, step * rows : (step + 1) * rows],
                grads[...],
                preferred_element_type=jnp.float32,
            )
        out[low : low + tile] = total.astype(jnp.bfloat16)


def weight_pass(inputs, gathered):
    width, tokens = inputs.shape
    columns = gathered[0].shape[1]
    return pl.pallas_call(
        weight_kernel,
        out_shape=jax.ShapeDtypeStruct((width, columns), jnp.bfloat16),
        in_specs=vmem(1 + len(gathered)),
        out_specs=pl.BlockSpec(memory_space=pltpu.VMEM),
        cost_estimate=pl.CostEstimate(
            flops=2 * tokens * width * columns, transcendentals=0, bytes_accessed=4 << 20
        ),
        compiler_params=ROOM,
        name="weight_pass",
    )(inputs, *gathered)


def steps(query_rows, key_rows, value_rows, out_grad, inputs):
    rows, features = query_rows.shape
    sizes = tuple(lax.axis_size(name) for name in AXES)
    ny, nx, nz, nc = sizes
    devices = ny * nx * nz * nc
    scale = 1.0 / math.sqrt(HEAD)
    core = lax.axis_index("c").astype(jnp.int32)
    parity = lax.rem(lax.axis_index("z").astype(jnp.int32), 2)
    place = jnp.stack([core, parity, lax.axis_index("y").astype(jnp.int32)])
    even = core == 0
    place, even, query_rows = lax.optimization_barrier((place, even, query_rows))

    def both_halves(mine, other):
        return jnp.where(
            even, jnp.concatenate([mine, other], 1), jnp.concatenate([other, mine], 1)
        )

    def swaps(one, two):
        got_one = swap(one, devices, 0)
        got_two = swap(two, devices, 1)
        return got_one, got_two

    key_mine, key_other, mine, other = pack(place, key_rows, query_rows, out_grad, value_rows)
    key_part = to_core(key_other, devices)
    part = to_core(other, devices)
    (key,) = join(key_mine, key_part)
    first_k, second_k = swaps(key, key)
    keys = (first_k, key, second_k)
    query, grad, value = join(mine, part)
    first_v, second_v = swaps(value, value)

    inputs, _ = lax.optimization_barrier((inputs, mine))
    blocks = input_blocks(place, inputs, ny)
    taken = [blocks[0]]
    for step in range(1, ny):
        taken.append(along_y(blocks[step], sizes, step))

    first, own, second, lse = value_pass(place, query, grad, keys, scale)
    from_first, from_second = swaps(first, second)
    value_half = (own + from_first.astype(jnp.float32) + from_second.astype(jnp.float32)).astype(
        jnp.bfloat16
    )
    *taken, query, _ = lax.optimization_barrier((*taken, query, value_half))
    dq, dq_other, key_first, key_own, key_second = score_pass(
        place, query, grad, keys, (first_v, value, second_v), lse, scale
    )
    key_from_first, key_from_second = swaps(key_first, key_second)
    taken = stack(taken)
    taken_part = to_core(taken, devices)
    taken = merge(taken, taken_part)
    gathered = [value_half]
    for step in range(1, ny):
        gathered.append(along_y(value_half, sizes, step))
    partial = weight_pass(taken, gathered)
    value_back = to_core(value_half[rows:], devices)
    query_back = to_core(dq_other, devices)
    half = features // 2
    own_count = inputs.shape[1] // devices
    pieces = partial.reshape(nx * nz * nc, own_count, half)
    arrived = lax.all_to_all(pieces, ("x", "z", "c"), 0, 0, tiled=True)
    summed = jnp.sum(
        arrived.reshape(nx * nz, nc, own_count, half).astype(jnp.float32), axis=0
    )
    weight_grad = summed.transpose(1, 0, 2).reshape(own_count, features) * (
        1.0 / math.sqrt(rows * devices)
    )

    key_half = (
        key_own + key_from_first.astype(jnp.float32) + key_from_second.astype(jnp.float32)
    ).astype(jnp.bfloat16)
    key_back = to_core(key_half[rows:], devices)
    query_grad = both_halves(dq, query_back)
    value_grad = both_halves(value_half[:rows], value_back)
    key_grad = both_halves(key_half[:rows], key_back)
    return (query_grad, key_grad, value_grad, weight_grad)


def solution(mesh):
    fine = physical_mesh(mesh)
    spec = P(AXES, None)
    return jax.shard_map(
        steps,
        mesh=fine,
        in_specs=(spec,) * 5,
        out_specs=(spec,) * 4,
        check_vma=False,
    )
```

```python
import math

import jax
import jax.numpy as jnp
from jax import lax
from jax.experimental import pallas as pl
from jax.experimental.pallas import tpu as pltpu
from jax.sharding import Mesh, PartitionSpec as P


HEAD = 128
NEG = -1e30
ROOM = pltpu.CompilerParams(vmem_limit_bytes=20 << 20)


AXES = ("y", "x", "z", "c")
LAST = (((1,), (1,)), ((), ()))
FIRST = (((0,), (0,)), ((), ()))


def physical_mesh(mesh):
    count = mesh.devices.size
    sizes = (4, 4, 8, 2) if count == 256 else (2, count // 8, 2, 2)
    return Mesh(mesh.devices.reshape(sizes), AXES)


def to_core(array, count):
    return lax.ppermute(array, AXES, [(device, device ^ 1) for device in range(count)])


def swap(array, count, odd):
    chips = count // 2
    pairs = []
    for device in range(count):
        chip, core = device // 2, device % 2
        other = ((chip - odd) ^ 1) + odd
        pairs.append((device, other % chips * 2 + core))
    return lax.ppermute(array, AXES, pairs)


def along_y(array, sizes, step):
    ny, nx, nz, nc = sizes
    rest = nx * nz * nc
    pairs = [(device, (device + step * rest) % (ny * rest)) for device in range(ny * rest)]
    return lax.ppermute(array, AXES, pairs)


def vmem(count):
    return [pl.BlockSpec(memory_space=pltpu.VMEM)] * count


def pack_kernel(key, query, grad, value, key_mine, key_other, mine, other, bias, done):
    half = query.shape[1] // 2
    core = lax.axis_index("c")
    here = pl.multiple_of(core * half, half)
    there = pl.multiple_of((1 - core) * half, half)
    moves = [(key, key_other.at[0], there), (key, key_mine.at[0], here)]
    for at, source in enumerate((query, grad, value)):
        moves += [(source, other.at[at], there), (source, mine.at[at], here)]
    copies = [
        pltpu.make_async_copy(source.at[:, pl.ds(start, half)], target, done.at[at])
        for at, (source, target, start) in enumerate(moves)
    ]
    for copy in copies:
        copy.start()
    window_bias(core == lax.rem(lax.axis_index("z"), 2), bias)
    for copy in copies:
        copy.wait()


def pack(key, query, grad, value):
    rows, features = query.shape
    one, three = (
        jax.ShapeDtypeStruct((count, rows, features // 2), query.dtype) for count in (1, 3)
    )
    return pl.pallas_call(
        pack_kernel,
        out_shape=(one, one, three, three, jax.ShapeDtypeStruct((8, 2 * rows), jnp.float32)),
        in_specs=[pl.BlockSpec(memory_space=pltpu.HBM)] * 4,
        out_specs=tuple(vmem(5)),
        scratch_shapes=[pltpu.SemaphoreType.DMA((8,))],
        compiler_params=ROOM,
        name="pack",
    )(*(in_hbm(array) for array in (key, query, grad, value)))


def in_hbm(array):
    return pltpu.with_memory_space_constraint(array, pltpu.HBM)


def join_kernel(mine, part, *targets):
    rows = mine.shape[1]
    for at, target in enumerate(targets):
        target[:rows] = mine[at]
        target[rows:] = part[at]


def join(mine, part):
    count, rows, half = mine.shape
    two = jax.ShapeDtypeStruct((2 * rows, half), mine.dtype)
    return pl.pallas_call(
        join_kernel,
        out_shape=(two,) * count,
        in_specs=vmem(2),
        out_specs=tuple(vmem(count)),
        compiler_params=ROOM,
        name="join",
    )(mine, part)


def window_bias(alike, out):
    shape = out.shape[:0] + (1, out.shape[1])
    left = lax.broadcasted_iota(jnp.int32, shape, 1) < out.shape[1] // 2
    unlike = jnp.where(alike, 0.0, NEG)
    like = jnp.where(alike, NEG, 0.0)
    out[0:1] = jnp.where(left, 0.0, unlike)
    out[1:2] = jnp.where(left, like, 0.0)
    out[2:3] = jnp.zeros(shape, jnp.float32)
    out[3:4] = jnp.zeros(shape, jnp.float32)
    out[4:5] = jnp.where(left, 0.0, like)
    out[5:6] = jnp.where(left, unlike, 0.0)
    out[6:8] = jnp.zeros((2, out.shape[1]), jnp.float32)


def scores_of(bias, keys, queries, scale):
    flat = lax.dot_general(keys, queries, LAST, preferred_element_type=jnp.float32) * scale
    size = flat.shape[0] // 6
    parts = []
    for block in range(6):
        part = flat[block * size : (block + 1) * size]
        parts.append(part + bias[block : block + 1] if block in (0, 1, 4, 5) else part)
    return jnp.concatenate(parts, 0)


def value_kernel(scale, bias, query, grad, first_k, key, second_k, first, own, second, lse):
    two, width = query.shape
    for head in range(width // HEAD):
        at = slice(head * HEAD, (head + 1) * HEAD)
        keys = jnp.concatenate([first_k[:, at], key[:, at], second_k[:, at]], 0)
        scores = scores_of(bias, keys, query[:, at], scale)
        top = jnp.max(scores, axis=0, keepdims=True)
        raised = jnp.exp(scores - top)
        total = jnp.sum(raised, axis=0, keepdims=True)
        probs = (raised * (1.0 / total)).astype(jnp.bfloat16)
        terms = jnp.dot(probs, grad[:, at], preferred_element_type=jnp.float32)
        first[:, at] = terms[:two].astype(jnp.bfloat16)
        own[:, at] = terms[two : 2 * two]
        second[:, at] = terms[2 * two :].astype(jnp.bfloat16)
        lse[head] = jnp.broadcast_to(top + jnp.log(total), lse.shape[1:])


def score_kernel(
    scale, bias, query, grad, first_k, key, second_k, first_v, value, second_v, lse,
    query_grad, query_back, first, own, second,
):
    two, width = query.shape
    for head in range(width // HEAD):
        at = slice(head * HEAD, (head + 1) * HEAD)
        keys = jnp.concatenate([first_k[:, at], key[:, at], second_k[:, at]], 0)
        values = jnp.concatenate([first_v[:, at], value[:, at], second_v[:, at]], 0)
        scores = scores_of(bias, keys, query[:, at], scale)
        probs = jnp.exp(scores - lse[head, 0:1])
        grad_probs = lax.dot_general(values, grad[:, at], LAST, preferred_element_type=jnp.float32)
        rounded = probs.astype(jnp.bfloat16).astype(jnp.float32)
        delta = jnp.sum(rounded * grad_probs, axis=0, keepdims=True)
        low = (probs * (grad_probs - delta)).astype(jnp.bfloat16)
        turned = lax.dot_general(keys, low, FIRST, preferred_element_type=jnp.float32) * scale
        found = turned.T.astype(jnp.bfloat16)
        query_grad[:, at] = found[: two // 2]
        query_back[:, at] = found[two // 2 :]
        terms = jnp.dot(low, query[:, at], preferred_element_type=jnp.float32) * scale
        first[:, at] = terms[:two].astype(jnp.bfloat16)
        own[:, at] = terms[two : 2 * two]
        second[:, at] = terms[2 * two :].astype(jnp.bfloat16)


def value_pass(bias, query, grad, keys, scale):
    two, width = query.shape
    heads = width // HEAD
    low = jax.ShapeDtypeStruct((two, width), jnp.bfloat16)
    high = jax.ShapeDtypeStruct((two, width), jnp.float32)
    work = heads * two * 3 * two
    return pl.pallas_call(
        lambda *refs: value_kernel(scale, *refs),
        out_shape=(low, high, low, jax.ShapeDtypeStruct((heads, 8, two), jnp.float32)),
        in_specs=vmem(6),
        out_specs=tuple(vmem(4)),
        cost_estimate=pl.CostEstimate(
            flops=4 * work * HEAD, transcendentals=work, bytes_accessed=4 << 20
        ),
        compiler_params=ROOM,
        name="value_pass",
    )(bias, query, grad, *keys)


def score_pass(bias, query, grad, keys, values, lse, scale):
    two, width = query.shape
    heads = width // HEAD
    low = jax.ShapeDtypeStruct((two, width), jnp.bfloat16)
    high = jax.ShapeDtypeStruct((two, width), jnp.float32)
    part = jax.ShapeDtypeStruct((two // 2, width), jnp.bfloat16)
    work = heads * two * 3 * two
    return pl.pallas_call(
        lambda *refs: score_kernel(scale, *refs),
        out_shape=(part, part, low, high, low),
        in_specs=vmem(10),
        out_specs=tuple(vmem(5)),
        cost_estimate=pl.CostEstimate(
            flops=8 * work * HEAD, transcendentals=work, bytes_accessed=6 << 20
        ),
        compiler_params=ROOM,
        name="score_pass",
    )(bias, query, grad, *keys, *values, lse)


def block_kernel(count, own, *blocks):
    size = own.shape[1] // count
    for step, block in enumerate(blocks):
        target = lax.rem(lax.axis_index("y") + step, count)
        block[...] = own[:, pl.ds(pl.multiple_of(target * size, size), size)]


def input_blocks(own, count):
    rows, width = own.shape
    block = jax.ShapeDtypeStruct((rows, width // count), own.dtype)
    return pl.pallas_call(
        lambda *refs: block_kernel(count, *refs),
        out_shape=(block,) * count,
        in_specs=vmem(1),
        out_specs=tuple(vmem(count)),
        compiler_params=ROOM,
        name="input_blocks",
    )(own)


def stack_kernel(count, *refs):
    for step in range(count):
        refs[count][step] = refs[step][...]


def stack(blocks):
    count = len(blocks)
    return pl.pallas_call(
        lambda *refs: stack_kernel(count, *refs),
        out_shape=jax.ShapeDtypeStruct((count,) + blocks[0].shape, blocks[0].dtype),
        in_specs=vmem(count),
        out_specs=pl.BlockSpec(memory_space=pltpu.VMEM),
        compiler_params=ROOM,
        name="stack",
    )(*blocks)


def merge_kernel(own, part, out):
    count, rows, _ = own.shape
    for step in range(count):
        at = 2 * step * rows
        out[:, at : at + rows] = own[step].T
        out[:, at + rows : at + 2 * rows] = part[step].T


def merge(own, part):
    count, rows, width = own.shape
    return pl.pallas_call(
        merge_kernel,
        out_shape=jax.ShapeDtypeStruct((width, 2 * count * rows), own.dtype),
        in_specs=vmem(2),
        out_specs=pl.BlockSpec(memory_space=pltpu.VMEM),
        compiler_params=ROOM,
        name="merge",
    )(own, part)


def weight_kernel(inputs, *refs):
    gathered, out = refs[:-1], refs[-1]
    rows = gathered[0].shape[0]
    tile = 256
    for low in range(0, out.shape[0], tile):
        total = jnp.zeros((tile, out.shape[1]), jnp.float32)
        for step, grads in enumerate(gathered):
            total += jnp.dot(
                inputs[low : low + tile, step * rows : (step + 1) * rows],
                grads[...],
                preferred_element_type=jnp.float32,
            )
        out[low : low + tile] = total.astype(jnp.bfloat16)


def weight_pass(inputs, gathered):
    width, tokens = inputs.shape
    columns = gathered[0].shape[1]
    return pl.pallas_call(
        weight_kernel,
        out_shape=jax.ShapeDtypeStruct((width, columns), jnp.bfloat16),
        in_specs=vmem(1 + len(gathered)),
        out_specs=pl.BlockSpec(memory_space=pltpu.VMEM),
        cost_estimate=pl.CostEstimate(
            flops=2 * tokens * width * columns, transcendentals=0, bytes_accessed=4 << 20
        ),
        compiler_params=ROOM,
        name="weight_pass",
    )(inputs, *gathered)


def steps(query_rows, key_rows, value_rows, out_grad, inputs):
    rows, features = query_rows.shape
    sizes = tuple(lax.axis_size(name) for name in AXES)
    ny, nx, nz, nc = sizes
    devices = ny * nx * nz * nc
    scale = 1.0 / math.sqrt(HEAD)
    even = lax.axis_index("c") == 0
    even, query_rows = lax.optimization_barrier((even, query_rows))

    def both_halves(mine, other):
        return jnp.where(
            even, jnp.concatenate([mine, other], 1), jnp.concatenate([other, mine], 1)
        )

    def swaps(one, two):
        got_one = swap(one, devices, 0)
        got_two = swap(two, devices, 1)
        return got_one, got_two

    key_mine, key_other, mine, other, bias = pack(key_rows, query_rows, out_grad, value_rows)
    key_part = to_core(key_other, devices)
    part = to_core(other, devices)
    (key,) = join(key_mine, key_part)
    first_k, second_k = swaps(key, key)
    keys = (first_k, key, second_k)
    query, grad, value = join(mine, part)
    first_v, second_v = swaps(value, value)

    inputs, _ = lax.optimization_barrier((inputs, mine))
    blocks = input_blocks(inputs, ny)
    taken = [blocks[0]]
    for step in range(1, ny):
        taken.append(along_y(blocks[step], sizes, step))

    first, own, second, lse = value_pass(bias, query, grad, keys, scale)
    from_first, from_second = swaps(first, second)
    value_half = (own + from_first.astype(jnp.float32) + from_second.astype(jnp.float32)).astype(
        jnp.bfloat16
    )
    query, _ = lax.optimization_barrier((query, value_half))
    dq, dq_other, key_first, key_own, key_second = score_pass(
        bias, query, grad, keys, (first_v, value, second_v), lse, scale
    )
    key_from_first, key_from_second = swaps(key_first, key_second)
    *taken, _ = lax.optimization_barrier((*taken, key_own))
    taken = stack(taken)
    taken_part = to_core(taken, devices)
    taken = merge(taken, taken_part)
    gathered = [value_half]
    for step in range(1, ny):
        gathered.append(along_y(value_half, sizes, step))
    partial = weight_pass(taken, gathered)
    value_back = to_core(value_half[rows:], devices)
    query_back = to_core(dq_other, devices)
    half = features // 2
    own_count = inputs.shape[1] // devices
    pieces = partial.reshape(nx * nz * nc, own_count, half)
    arrived = lax.all_to_all(pieces, ("x", "z", "c"), 0, 0, tiled=True)
    summed = jnp.sum(
        arrived.reshape(nx * nz, nc, own_count, half).astype(jnp.float32), axis=0
    )
    weight_grad = summed.transpose(1, 0, 2).reshape(own_count, features) * (
        1.0 / math.sqrt(rows * devices)
    )

    key_half = (
        key_own + key_from_first.astype(jnp.float32) + key_from_second.astype(jnp.float32)
    ).astype(jnp.bfloat16)
    key_back = to_core(key_half[rows:], devices)
    query_grad = both_halves(dq, query_back)
    value_grad = both_halves(value_half[:rows], value_back)
    key_grad = both_halves(key_half[:rows], key_back)
    return (query_grad, key_grad, value_grad, weight_grad)


def solution(mesh):
    fine = physical_mesh(mesh)
    spec = P(AXES, None)
    return jax.shard_map(
        steps,
        mesh=fine,
        in_specs=(spec,) * 5,
        out_specs=(spec,) * 4,
        check_vma=False,
    )
```

```python
import math

import jax
import jax.numpy as jnp
from jax import lax
from jax.experimental import pallas as pl
from jax.experimental.pallas import tpu as pltpu
from jax.sharding import Mesh, PartitionSpec as P


HEAD = 128
NEG = -1e30
LOG2E = 1.0 / math.log(2.0)
ROOM = pltpu.CompilerParams(vmem_limit_bytes=20 << 20)


AXES = ("y", "x", "z", "c")
LAST = (((1,), (1,)), ((), ()))
FIRST = (((0,), (0,)), ((), ()))


def physical_mesh(mesh):
    count = mesh.devices.size
    sizes = (4, 4, 8, 2) if count == 256 else (2, count // 8, 2, 2)
    return Mesh(mesh.devices.reshape(sizes), AXES)


def to_core(array, count):
    return lax.ppermute(array, AXES, [(device, device ^ 1) for device in range(count)])


def swap(array, count, odd):
    chips = count // 2
    pairs = []
    for device in range(count):
        chip, core = device // 2, device % 2
        other = ((chip - odd) ^ 1) + odd
        pairs.append((device, other % chips * 2 + core))
    return lax.ppermute(array, AXES, pairs)


def along_y(array, sizes, step):
    ny, nx, nz, nc = sizes
    rest = nx * nz * nc
    pairs = [(device, (device + step * rest) % (ny * rest)) for device in range(ny * rest)]
    return lax.ppermute(array, AXES, pairs)


def vmem(count):
    return [pl.BlockSpec(memory_space=pltpu.VMEM)] * count


def pack_kernel(key, query, grad, value, key_mine, key_other, mine, other, bias, done):
    half = query.shape[1] // 2
    core = lax.axis_index("c")
    here = pl.multiple_of(core * half, half)
    there = pl.multiple_of((1 - core) * half, half)
    moves = [(key, key_other.at[0], there), (key, key_mine.at[0], here)]
    for at, source in enumerate((query, grad, value)):
        moves += [(source, other.at[at], there), (source, mine.at[at], here)]
    copies = [
        pltpu.make_async_copy(source.at[:, pl.ds(start, half)], target, done.at[at])
        for at, (source, target, start) in enumerate(moves)
    ]
    for copy in copies:
        copy.start()
    window_bias(core == lax.rem(lax.axis_index("z"), 2), bias)
    for copy in copies:
        copy.wait()


def pack(key, query, grad, value):
    rows, features = query.shape
    one, three = (
        jax.ShapeDtypeStruct((count, rows, features // 2), query.dtype) for count in (1, 3)
    )
    return pl.pallas_call(
        pack_kernel,
        out_shape=(one, one, three, three, jax.ShapeDtypeStruct((8, 2 * rows), jnp.float32)),
        in_specs=[pl.BlockSpec(memory_space=pltpu.HBM)] * 4,
        out_specs=tuple(vmem(5)),
        scratch_shapes=[pltpu.SemaphoreType.DMA((8,))],
        compiler_params=ROOM,
        name="pack",
    )(*(in_hbm(array) for array in (key, query, grad, value)))


def in_hbm(array):
    return pltpu.with_memory_space_constraint(array, pltpu.HBM)


def join_kernel(mine, part, *targets):
    rows = mine.shape[1]
    for at, target in enumerate(targets):
        target[:rows] = mine[at]
        target[rows:] = part[at]


def join(mine, part):
    count, rows, half = mine.shape
    two = jax.ShapeDtypeStruct((2 * rows, half), mine.dtype)
    return pl.pallas_call(
        join_kernel,
        out_shape=(two,) * count,
        in_specs=vmem(2),
        out_specs=tuple(vmem(count)),
        compiler_params=ROOM,
        name="join",
    )(mine, part)


def window_bias(alike, out):
    shape = out.shape[:0] + (1, out.shape[1])
    left = lax.broadcasted_iota(jnp.int32, shape, 1) < out.shape[1] // 2
    unlike = jnp.where(alike, 0.0, NEG)
    like = jnp.where(alike, NEG, 0.0)
    out[0:1] = jnp.where(left, 0.0, unlike)
    out[1:2] = jnp.where(left, like, 0.0)
    out[2:3] = jnp.zeros(shape, jnp.float32)
    out[3:4] = jnp.zeros(shape, jnp.float32)
    out[4:5] = jnp.where(left, 0.0, like)
    out[5:6] = jnp.where(left, unlike, 0.0)
    out[6:8] = jnp.zeros((2, out.shape[1]), jnp.float32)


def scores_of(bias, keys, queries, scale):
    flat = lax.dot_general(keys, queries, LAST, preferred_element_type=jnp.float32) * scale
    size = flat.shape[0] // 6
    parts = []
    for block in range(6):
        part = flat[block * size : (block + 1) * size]
        parts.append(part + bias[block : block + 1] if block in (0, 1, 4, 5) else part)
    return jnp.concatenate(parts, 0)


def value_kernel(scale, bias, query, grad, first_k, key, second_k, first, own, second, lse):
    two, width = query.shape
    for head in range(width // HEAD):
        at = slice(head * HEAD, (head + 1) * HEAD)
        keys = jnp.concatenate([first_k[:, at], key[:, at], second_k[:, at]], 0)
        scores = scores_of(bias, keys, query[:, at], scale * LOG2E)
        top = jnp.max(scores, axis=0, keepdims=True)
        raised = jnp.exp2(scores - top)
        total = jnp.sum(raised, axis=0, keepdims=True)
        probs = (raised * (1.0 / total)).astype(jnp.bfloat16)
        terms = jnp.dot(probs, grad[:, at], preferred_element_type=jnp.float32)
        first[:, at] = terms[:two].astype(jnp.bfloat16)
        own[:, at] = terms[two : 2 * two]
        second[:, at] = terms[2 * two :].astype(jnp.bfloat16)
        lse[head] = jnp.broadcast_to(top + jnp.log(total) * LOG2E, lse.shape[1:])


def score_kernel(
    scale, bias, query, grad, first_k, key, second_k, first_v, value, second_v, lse,
    query_grad, query_back, first, own, second,
):
    two, width = query.shape
    for head in range(width // HEAD):
        at = slice(head * HEAD, (head + 1) * HEAD)
        keys = jnp.concatenate([first_k[:, at], key[:, at], second_k[:, at]], 0)
        values = jnp.concatenate([first_v[:, at], value[:, at], second_v[:, at]], 0)
        scores = scores_of(bias, keys, query[:, at], scale * LOG2E)
        probs = jnp.exp2(scores - lse[head, 0:1])
        grad_probs = lax.dot_general(values, grad[:, at], LAST, preferred_element_type=jnp.float32)
        rounded = probs.astype(jnp.bfloat16).astype(jnp.float32)
        delta = jnp.sum(rounded * grad_probs, axis=0, keepdims=True)
        low = (probs * (grad_probs - delta)).astype(jnp.bfloat16)
        turned = lax.dot_general(keys, low, FIRST, preferred_element_type=jnp.float32) * scale
        found = turned.T.astype(jnp.bfloat16)
        query_grad[:, at] = found[: two // 2]
        query_back[:, at] = found[two // 2 :]
        terms = jnp.dot(low, query[:, at], preferred_element_type=jnp.float32) * scale
        first[:, at] = terms[:two].astype(jnp.bfloat16)
        own[:, at] = terms[two : 2 * two]
        second[:, at] = terms[2 * two :].astype(jnp.bfloat16)


def value_pass(bias, query, grad, keys, scale):
    two, width = query.shape
    heads = width // HEAD
    low = jax.ShapeDtypeStruct((two, width), jnp.bfloat16)
    high = jax.ShapeDtypeStruct((two, width), jnp.float32)
    work = heads * two * 3 * two
    return pl.pallas_call(
        lambda *refs: value_kernel(scale, *refs),
        out_shape=(low, high, low, jax.ShapeDtypeStruct((heads, 8, two), jnp.float32)),
        in_specs=vmem(6),
        out_specs=tuple(vmem(4)),
        cost_estimate=pl.CostEstimate(
            flops=4 * work * HEAD, transcendentals=work, bytes_accessed=4 << 20
        ),
        compiler_params=ROOM,
        name="value_pass",
    )(bias, query, grad, *keys)


def score_pass(bias, query, grad, keys, values, lse, scale):
    two, width = query.shape
    heads = width // HEAD
    low = jax.ShapeDtypeStruct((two, width), jnp.bfloat16)
    high = jax.ShapeDtypeStruct((two, width), jnp.float32)
    part = jax.ShapeDtypeStruct((two // 2, width), jnp.bfloat16)
    work = heads * two * 3 * two
    return pl.pallas_call(
        lambda *refs: score_kernel(scale, *refs),
        out_shape=(part, part, low, high, low),
        in_specs=vmem(10),
        out_specs=tuple(vmem(5)),
        cost_estimate=pl.CostEstimate(
            flops=8 * work * HEAD, transcendentals=work, bytes_accessed=6 << 20
        ),
        compiler_params=ROOM,
        name="score_pass",
    )(bias, query, grad, *keys, *values, lse)


def block_kernel(count, own, *blocks):
    size = own.shape[1] // count
    for step, block in enumerate(blocks):
        target = lax.rem(lax.axis_index("y") + step, count)
        block[...] = own[:, pl.ds(pl.multiple_of(target * size, size), size)]


def input_blocks(own, count):
    rows, width = own.shape
    block = jax.ShapeDtypeStruct((rows, width // count), own.dtype)
    return pl.pallas_call(
        lambda *refs: block_kernel(count, *refs),
        out_shape=(block,) * count,
        in_specs=vmem(1),
        out_specs=tuple(vmem(count)),
        compiler_params=ROOM,
        name="input_blocks",
    )(own)


def stack_kernel(count, *refs):
    for step in range(count):
        refs[count][step] = refs[step][...]


def stack(blocks):
    count = len(blocks)
    return pl.pallas_call(
        lambda *refs: stack_kernel(count, *refs),
        out_shape=jax.ShapeDtypeStruct((count,) + blocks[0].shape, blocks[0].dtype),
        in_specs=vmem(count),
        out_specs=pl.BlockSpec(memory_space=pltpu.VMEM),
        compiler_params=ROOM,
        name="stack",
    )(*blocks)


def merge_kernel(own, part, out):
    count, rows, _ = own.shape
    for step in range(count):
        at = 2 * step * rows
        out[:, at : at + rows] = own[step].T
        out[:, at + rows : at + 2 * rows] = part[step].T


def merge(own, part):
    count, rows, width = own.shape
    return pl.pallas_call(
        merge_kernel,
        out_shape=jax.ShapeDtypeStruct((width, 2 * count * rows), own.dtype),
        in_specs=vmem(2),
        out_specs=pl.BlockSpec(memory_space=pltpu.VMEM),
        compiler_params=ROOM,
        name="merge",
    )(own, part)


def weight_kernel(inputs, *refs):
    gathered, out = refs[:-1], refs[-1]
    grads = jnp.concatenate([part[...] for part in gathered], 0)
    tile = 256
    for low in range(0, out.shape[0], tile):
        total = jnp.dot(inputs[low : low + tile], grads, preferred_element_type=jnp.float32)
        out[low : low + tile] = total.astype(jnp.bfloat16)


def weight_pass(inputs, gathered):
    width, tokens = inputs.shape
    columns = gathered[0].shape[1]
    return pl.pallas_call(
        weight_kernel,
        out_shape=jax.ShapeDtypeStruct((width, columns), jnp.bfloat16),
        in_specs=vmem(1 + len(gathered)),
        out_specs=pl.BlockSpec(memory_space=pltpu.VMEM),
        cost_estimate=pl.CostEstimate(
            flops=2 * tokens * width * columns, transcendentals=0, bytes_accessed=4 << 20
        ),
        compiler_params=ROOM,
        name="weight_pass",
    )(inputs, *gathered)


def steps(query_rows, key_rows, value_rows, out_grad, inputs):
    rows, features = query_rows.shape
    sizes = tuple(lax.axis_size(name) for name in AXES)
    ny, nx, nz, nc = sizes
    devices = ny * nx * nz * nc
    scale = 1.0 / math.sqrt(HEAD)
    even = lax.axis_index("c") == 0
    even, query_rows = lax.optimization_barrier((even, query_rows))

    def both_halves(mine, other):
        return jnp.where(
            even, jnp.concatenate([mine, other], 1), jnp.concatenate([other, mine], 1)
        )

    def swaps(one, two):
        got_one = swap(one, devices, 0)
        got_two = swap(two, devices, 1)
        return got_one, got_two

    key_mine, key_other, mine, other, bias = pack(key_rows, query_rows, out_grad, value_rows)
    key_part = to_core(key_other, devices)
    part = to_core(other, devices)
    (key,) = join(key_mine, key_part)
    first_k, second_k = swaps(key, key)
    keys = (first_k, key, second_k)
    query, grad, value = join(mine, part)
    first_v, second_v = swaps(value, value)

    inputs, _ = lax.optimization_barrier((inputs, mine))
    blocks = input_blocks(inputs, ny)
    taken = [blocks[0]]
    for step in range(1, ny):
        taken.append(along_y(blocks[step], sizes, step))

    first, own, second, lse = value_pass(bias, query, grad, keys, scale)
    from_first, from_second = swaps(first, second)
    value_half = (own + from_first.astype(jnp.float32) + from_second.astype(jnp.float32)).astype(
        jnp.bfloat16
    )
    query, _ = lax.optimization_barrier((query, value_half))
    dq, dq_other, key_first, key_own, key_second = score_pass(
        bias, query, grad, keys, (first_v, value, second_v), lse, scale
    )
    key_from_first, key_from_second = swaps(key_first, key_second)
    *taken, _ = lax.optimization_barrier((*taken, key_own))
    taken = stack(taken)
    taken_part = to_core(taken, devices)
    taken = merge(taken, taken_part)
    gathered = [value_half]
    for step in range(1, ny):
        gathered.append(along_y(value_half, sizes, step))
    partial = weight_pass(taken, gathered)
    value_back = to_core(value_half[rows:], devices)
    query_back = to_core(dq_other, devices)
    half = features // 2
    own_count = inputs.shape[1] // devices
    pieces = partial.reshape(nx * nz * nc, own_count, half)
    arrived = lax.all_to_all(pieces, ("x", "z", "c"), 0, 0, tiled=True)
    summed = jnp.sum(
        arrived.reshape(nx * nz, nc, own_count, half).astype(jnp.float32), axis=0
    )
    weight_grad = summed.transpose(1, 0, 2).reshape(own_count, features) * (
        1.0 / math.sqrt(rows * devices)
    )

    key_half = (
        key_own + key_from_first.astype(jnp.float32) + key_from_second.astype(jnp.float32)
    ).astype(jnp.bfloat16)
    key_back = to_core(key_half[rows:], devices)
    query_grad = both_halves(dq, query_back)
    value_grad = both_halves(value_half[:rows], value_back)
    key_grad = both_halves(key_half[:rows], key_back)
    return (query_grad, key_grad, value_grad, weight_grad)


def solution(mesh):
    fine = physical_mesh(mesh)
    spec = P(AXES, None)
    return jax.shard_map(
        steps,
        mesh=fine,
        in_specs=(spec,) * 5,
        out_specs=(spec,) * 4,
        check_vma=False,
    )
```
